32 devices in a mesh: dp: 4 (over z), tensor: 2 (over core), shard: 4 (over y, x).
Axes of the slice: x: 2, y: 2, z: 4, core: 2. Of those that a mesh axis runs over, the one named last changes fastest.
Arguments:
- weights: float32 [2, 896, 4864], P(None, 'dp', 'tensor'), may hold values from -0.1875 to 0.1875
- grads: float32 [4, 2, 896, 4864], P('dp', None, None, ('tensor', 'shard')), may hold values from -40 to 40, as said below
- bases: float32 [2, 896, 256], replicated, may hold values from -3 to 3
- first_moment: float32 [2, 256, 4864], P(None, None, ('tensor', 'shard')), may hold values from -0.12 to 0.12
- second_moment: float32 [2, 256, 4864], P(None, None, ('tensor', 'shard')), may hold values from 1e-05 to 0.001
- gain: float32 [896], replicated, may hold values from 0.5 to 1.5
- gain_grad: float32 [4, 896], P('dp'), may hold values from -384 to 384
- gain_first: float32 [896], replicated, may hold values from -3 to 3
- gain_second: float32 [896], replicated, may hold values from 0.01 to 1
Outputs:
- new_weights: float32 [2, 896, 4864], P(None, 'dp', 'tensor')
- new_bases: float32 [2, 896, 256], replicated
- new_first: float32 [2, 256, 4864], P(None, None, ('tensor', 'shard'))
- new_second: float32 [2, 256, 4864], P(None, None, ('tensor', 'shard'))
- new_gain: float32 [896], replicated
- new_gain_first: float32 [896], replicated
- new_gain_second: float32 [896], replicated
The draws below stay inside these ranges and needn't reach their ends.
Inputs may be any that keep to these rules, and one draw needn't show every extreme that they name: `grads`: partial gradients of the data-parallel replicas.
All inputs are finite; a program needn't handle non-finite values.
Results may differ from the reference program's by a relative error of at most 0.0001.
Values sent between devices are 32-bit elements; how exact they have to be, the bound alone decides.
A program may use at most 128 MiB of HBM per device.

```python
import math
import jax
import jax.numpy as jnp
from jax import lax

D = 896
FF = 4864
R = 256
MATS = 2
NS_STEPS = 5
REPLICAS = 4


def shared_factors(key, spread):
    key_entries, key_rows = jax.random.split(jax.random.fold_in(key, 17))
    raw_entries = jnp.clip(jax.random.normal(key_entries, (MATS, D, R), jnp.float32), -6.0, 6.0)
    row_scale = jnp.exp(jax.random.uniform(key_rows, (MATS, D, 1), jnp.float32, 0.0, spread))
    return (raw_entries, row_scale)


def pick_columns(columns, chosen):
    return jnp.take(columns, chosen, axis=1)


def draw_bases(key, part):
    spread = math.log(10.0)
    raw_entries, row_scale = shared_factors(key, spread)
    return (raw_entries * row_scale * (0.25 / math.sqrt(D))).astype(jnp.float32)


def draw_grads(key, part):
    spread = math.log(10.0)
    raw_entries, row_scale = shared_factors(key, spread)
    local_key = jax.random.fold_in(key, 5)
    key_scale, key_weight, key_pick, key_own = jax.random.split(local_key, 4)
    position = jnp.arange(FF, dtype=jnp.float32) / FF
    column_scale = jnp.exp(jax.random.uniform(key_scale, (MATS, 1, FF), jnp.float32, 0.0, math.log(30.0)))
    chosen_columns = jax.random.randint(key_pick, (MATS, FF), 0, R)
    picked = jax.vmap(pick_columns)(raw_entries * row_scale, chosen_columns)
    column_ramp = jnp.exp(0.5 * math.log(3.0) * position)
    column_weight = jnp.clip(jax.random.normal(key_weight, (MATS, 1, FF), jnp.float32), -4.0, 4.0)
    noise_part = jnp.clip(jax.random.normal(key_own, (REPLICAS, MATS, D, FF), jnp.float32), -6.0, 6.0)
    common_part = 1.5 * column_weight * picked
    own_part = noise_part * row_scale
    total = 0.003 * (common_part[None] + own_part) * column_ramp * column_scale
    return jnp.clip(total, -40.0, 40.0).astype(jnp.float32)


def steps_of(key, extent, shards, low, largest):
    level = 1.0
    for dim, shards_of in shards:
        heights = jax.random.uniform(jax.random.fold_in(jax.random.fold_in(key, 6), dim), (shards_of,), jnp.float32, low / len(shards), largest / len(shards))
        level = level * jnp.repeat(jnp.exp(heights), extent[dim] // shards_of).reshape((-1,) + (1,) * (len(extent) - 1 - dim))
    return level


def scatter_about(rng, shape, deviation, bound, shards=(), kind=jnp.bfloat16):
    entries = jax.random.normal(rng, shape, jnp.float32) * deviation
    if len(shards) > 0:
        entries = steps_of(rng, shape, shards, -0.22, 0.18) * entries
    return jnp.clip(entries, min=-bound, max=bound).astype(kind)


def setup_inputs(seed: int = 0) -> dict:
    seeds = jax.random.split(jax.random.key(seed), 10)
    weights = scatter_about(seeds[0], (MATS, D, FF), D ** -0.5, 0.1875, ((1, 4), (2, 2)), jnp.float32)
    grads = draw_grads(jax.random.fold_in(seeds[9], 71), 0)
    bases = draw_bases(jax.random.fold_in(seeds[9], 71), 0)
    first_moment = scatter_about(seeds[3], (MATS, R, FF), 0.02, 0.12, ((2, 8),), jnp.float32)
    second_moment = jnp.clip(jnp.exp(math.log(0.001) - 4.6051703 * jax.random.uniform(seeds[4], (MATS, R, FF), jnp.float32) ** steps_of(seeds[4], (MATS, R, FF), ((2, 8),), -0.2, 0.2)), 9.999999747378752e-06, 0.001)
    gain = jnp.clip(1.0 + 0.1 * jax.random.normal(seeds[5], (D,), jnp.float32), 0.5, 1.5)
    gain_grad = scatter_about(seeds[6], (REPLICAS, D), (2 * D ** 0.5), 384.0, ((0, 4),), jnp.float32)
    gain_first = scatter_about(seeds[7], (D,), 0.5, 3.0, (), jnp.float32)
    gain_second = jnp.clip(jnp.exp(jax.random.uniform(seeds[8], (D,), jnp.float32, math.log(0.01), math.log(1.0))), 0.01, 1.0)
    return dict(weights=weights, grads=grads, bases=bases, first_moment=first_moment, second_moment=second_moment, gain=gain, gain_grad=gain_grad, gain_first=gain_first, gain_second=gain_second)


beta_one = 0.9
beta_two = 0.999
adam_eps = 1e-08
adam_step = 100
learn_rate = 0.02
galore_scale = 0.25
norm_eps = 1e-06

def product(left, right):
    return jnp.dot(left, right, precision=lax.Precision.HIGHEST, preferred_element_type=jnp.float32)

def reference(weights, grads, bases, first_moment, second_moment, gain, gain_grad, gain_first, gain_second):
    grad_total = lax.optimization_barrier(jnp.sum(grads, axis=0))
    gain_total = lax.optimization_barrier(jnp.sum(gain_grad, axis=0))
    squares = jnp.sum(grad_total * grad_total) + jnp.sum(gain_total * gain_total)
    clip_factor = jnp.minimum(1.0, math.sqrt(MATS * FF) / (jnp.sqrt(squares) + norm_eps))
    bias_one = 1.0 - beta_one ** adam_step
    bias_two = 1.0 - beta_two ** adam_step
    out_weights = []
    out_bases = []
    out_first = []
    out_second = []
    for matrix_id in range(MATS):
        matrix = grad_total[matrix_id]
        carried = product(matrix.T, bases[matrix_id])
        sketch = product(matrix, carried)
        newton_iterate = sketch / (jnp.sqrt(jnp.sum(sketch * sketch)) + norm_eps)
        for ns_turn in range(NS_STEPS):
            gram = product(newton_iterate.T, newton_iterate)
            newton_iterate = 1.5 * newton_iterate - 0.5 * product(newton_iterate, gram)
        projected_gradient = clip_factor * product(newton_iterate.T, matrix)
        first_new = beta_one * first_moment[matrix_id] + (1.0 - beta_one) * projected_gradient
        second_new = beta_two * second_moment[matrix_id] + (1.0 - beta_two) * projected_gradient * projected_gradient
        update_direction = first_new / bias_one / (jnp.sqrt(second_new / bias_two) + adam_eps)
        weight_delta = product(newton_iterate, update_direction)
        updated = weights[matrix_id] - learn_rate * galore_scale * weight_delta
        out_weights.append(updated)
        out_bases.append(newton_iterate)
        out_first.append(first_new)
        out_second.append(second_new)
    clipped_gain = clip_factor * gain_total
    gain_first_new = beta_one * gain_first + (1.0 - beta_one) * clipped_gain
    gain_second_new = beta_two * gain_second + (1.0 - beta_two) * clipped_gain * clipped_gain
    gain_new = gain - learn_rate * (gain_first_new / bias_one) / (jnp.sqrt(gain_second_new / bias_two) + adam_eps)
    return (jnp.stack(out_weights), jnp.stack(out_bases), jnp.stack(out_first), jnp.stack(out_second), gain_new, gain_first_new, gain_second_new)
```

```python
import functools
import math

import jax
import jax.numpy as jnp
from jax import lax
from jax.experimental import pallas as pl
from jax.experimental.pallas import tpu as pltpu
from jax.sharding import PartitionSpec as P

NS_STEPS = 5
MATS = 2

beta_one = 0.9
beta_two = 0.999
adam_eps = 1e-08
adam_step = 100
learn_rate = 0.02
galore_scale = 0.25
norm_eps = 1e-06

MESH = pl.DeviceIdType.MESH
VMEM = pl.BlockSpec(memory_space=pltpu.VMEM)
SKEW = 2


def dot(left, right, dims, precision=lax.Precision.HIGH):
    return lax.dot_general(
        left, right, (dims, ((), ())), precision=precision, preferred_element_type=jnp.float32
    )


def greet_line(dp, z):
    barrier = pltpu.get_barrier_semaphore()
    for k in range(1, dp):
        pl.semaphore_signal(
            barrier, inc=1, device_id={"dp": lax.rem(z + k, dp)}, device_id_type=MESH
        )
    pl.semaphore_wait(barrier, dp - 1)


def chunk_rows(rows, want):
    best = 8
    for size in range(8, want + 1, 8):
        if rows % size == 0:
            best = size
    return best


def line_sum_kernel(
    dp, ch, g_ref, gain_ref, out_ref, gain_out, rbuf, gbuf, send, recv, gsend, grecv
):
    z = lax.axis_index("dp")
    nch = g_ref.shape[1] // ch
    greet_line(dp, z)

    def remote(m, c, src, target):
        rows = pl.ds(c * ch, ch)
        return pltpu.make_async_remote_copy(
            src_ref=src.at[m, rows],
            dst_ref=rbuf.at[m, rows],
            send_sem=send.at[m, c],
            recv_sem=recv.at[m, c],
            device_id={"dp": target},
            device_id_type=MESH,
        )

    hops = (dp - 1 - z, z)
    target = (jnp.maximum(z - 1, 0), jnp.minimum(z + 1, dp - 1))

    def step(i, carry):
        for m in range(MATS):
            c = i - SKEW * hops[m]
            live = jnp.logical_and(c >= 0, c < nch)
            rows = pl.ds(pl.multiple_of(c * ch, 8), ch)

            @pl.when(jnp.logical_and(live, hops[m] == 0))
            def _():
                remote(m, c, g_ref, target[m]).start()

            @pl.when(jnp.logical_and(live, hops[m] > 0))
            def _():
                remote(m, c, rbuf, target[m]).wait_recv()

            @pl.when(jnp.logical_and(live, jnp.logical_and(hops[m] > 0, hops[m] < dp - 1)))
            def _():
                rbuf[m, rows, :] = rbuf[m, rows, :] + g_ref[m, rows, :]
                remote(m, c, rbuf, target[m]).start()

            @pl.when(jnp.logical_and(live, hops[m] == dp - 1))
            def _():
                out_ref[rows, :] = rbuf[m, rows, :] + g_ref[m, rows, :]

        return carry

    gcopies = []
    for k in range(1, dp):
        copy = pltpu.make_async_remote_copy(
            src_ref=gain_ref,
            dst_ref=gbuf.at[k],
            send_sem=gsend.at[k],
            recv_sem=grecv.at[k],
            device_id={"dp": lax.rem(z + k, dp)},
            device_id_type=MESH,
        )
        copy.start()
        gcopies.append(copy)

    lax.fori_loop(0, nch + SKEW * (dp - 1), step, 0)

    total = gain_ref[...]
    for k in range(1, dp):
        gcopies[k - 1].wait()
        total = total + gbuf[k]
    gain_out[...] = total

    @pl.when(jnp.logical_and(z > 0, z < dp - 1))
    def _():
        out_ref[...] = jnp.zeros_like(out_ref)

    def drain(c, carry):
        for m in range(MATS):

            @pl.when(hops[m] < dp - 1)
            def _():
                remote(m, c, rbuf, target[m]).wait_send()

        return carry

    lax.fori_loop(0, nch, drain, 0)


def line_sum(dp, grads, gain_grad):
    mats, rows, cols = grads.shape
    ch = chunk_rows(rows, 32)
    nch = rows // ch
    dma = pltpu.SemaphoreType.DMA
    return pl.pallas_call(
        functools.partial(line_sum_kernel, dp, ch),
        out_shape=(
            jax.ShapeDtypeStruct((rows, cols), jnp.float32),
            jax.ShapeDtypeStruct(gain_grad.shape, jnp.float32),
        ),
        in_specs=[VMEM, VMEM],
        out_specs=(VMEM, VMEM),
        scratch_shapes=[
            pltpu.VMEM((mats, rows, cols), jnp.float32),
            pltpu.VMEM((dp,) + gain_grad.shape, jnp.float32),
            dma((mats, nch)),
            dma((mats, nch)),
            dma((dp,)),
            dma((dp,)),
        ],
        compiler_params=pltpu.CompilerParams(
            collective_id=0, has_side_effects=True, vmem_limit_bytes=40 * 2**20
        ),
    )(grads, gain_grad)


def line_spread_kernel(dp, parts, *refs):
    n = len(parts)
    ins, outs = refs[:n], refs[n : 2 * n]
    send, recv, keep = refs[2 * n :]
    z = lax.axis_index("dp")
    greet_line(dp, z)
    hops = (z, dp - 1 - z)
    target = (jnp.minimum(z + 1, dp - 1), jnp.maximum(z - 1, 0))
    plan = [(a, r, ch) for a, (rows, ch) in enumerate(parts) for r in range(0, rows, ch)]

    def remote(m, k, first):
        a, r, ch = plan[k]
        dst = outs[a].at[m, pl.ds(r, ch)]
        return pltpu.make_async_remote_copy(
            src_ref=ins[a].at[pl.ds(r, ch)] if first else dst,
            dst_ref=dst,
            send_sem=send.at[m, k],
            recv_sem=recv.at[m, k],
            device_id={"dp": target[m]},
            device_id_type=MESH,
        )

    for m in range(MATS):

        @pl.when(hops[m] == 0)
        def _():
            for k in range(len(plan)):
                remote(m, k, True).start()
            for a in range(n):
                pltpu.make_async_copy(ins[a], outs[a].at[m], keep.at[a]).start()

    for i in range(len(plan) + SKEW * (dp - 1)):
        for m in range(MATS):
            for h in range(1, dp):
                k = i - SKEW * h
                if 0 <= k < len(plan):

                    @pl.when(hops[m] == h)
                    def _():
                        remote(m, k, False).wait_recv()
                        if h < dp - 1:
                            remote(m, k, False).start()

    for m in range(MATS):

        @pl.when(hops[m] == 0)
        def _():
            for a in range(n):
                pltpu.make_async_copy(ins[a], outs[a].at[m], keep.at[a]).wait()

        @pl.when(hops[m] < dp - 1)
        def _():
            for k in range(len(plan)):
                remote(m, k, False).wait_send()


def line_spread(dp, arrays, counts):
    parts = tuple((a.shape[0], a.shape[0] // c) for a, c in zip(arrays, counts))
    nk = sum(counts)
    dma = pltpu.SemaphoreType.DMA
    return pl.pallas_call(
        functools.partial(line_spread_kernel, dp, parts),
        out_shape=tuple(jax.ShapeDtypeStruct((MATS,) + a.shape, jnp.float32) for a in arrays),
        in_specs=[VMEM] * len(arrays),
        out_specs=tuple(VMEM for _ in arrays),
        scratch_shapes=[dma((MATS, nk)), dma((MATS, nk)), dma((len(arrays),))],
        compiler_params=pltpu.CompilerParams(
            collective_id=1, has_side_effects=True, vmem_limit_bytes=32 * 2**20
        ),
    )(*arrays)


def per_device(
    dp,
    weights,
    grads,
    bases,
    first_moment,
    second_moment,
    gain,
    gain_grad,
    gain_first,
    gain_second,
):
    z = lax.axis_index("dp")
    ff = first_moment.shape[2] * lax.axis_size(("tensor", "shard"))
    mine, gain_total = line_sum(dp, grads[0], gain_grad)
    gain_total = gain_total[0]
    basis = lax.dynamic_index_in_dim(bases, jnp.where(z * 2 >= dp, 1, 0), 0, keepdims=False)
    rows, rank = basis.shape
    local_squares = jnp.sum(mine * mine)
    carried = dot(mine, basis, ((0,), (0,)))
    partial = dot(mine, carried, ((1,), (0,)))
    packed = jnp.concatenate(
        [partial, jnp.full((8, rank), local_squares, jnp.float32)], axis=0
    )
    packed = lax.psum(packed, ("tensor", "shard"))
    sketch, squares = packed[:rows], packed[rows:, :128]
    iterate = sketch / (jnp.sqrt(jnp.sum(sketch * sketch)) + norm_eps)
    gram = dot(iterate, iterate, ((0,), (0,)))
    eye = jnp.eye(rank, dtype=jnp.float32)
    product = None
    for turn in range(NS_STEPS):
        factor = 1.5 * eye - 0.5 * gram
        product = factor if product is None else dot(product, factor, ((1,), (0,)))
        if turn < NS_STEPS - 1:
            gram = dot(dot(factor, gram, ((1,), (0,))), factor, ((1,), (0,)))
    new_basis = dot(iterate, product, ((1,), (0,)))
    projected = dot(new_basis, mine, ((0,), (0,)))
    projected, squares, new_bases = line_spread(dp, (projected, squares, new_basis), (8, 1, 7))

    total_squares = squares[0, 0, 0] + squares[1, 0, 0] + jnp.sum(gain_total * gain_total)
    clip_factor = jnp.minimum(1.0, math.sqrt(MATS * ff) / (jnp.sqrt(total_squares) + norm_eps))
    bias_one = 1.0 - beta_one**adam_step
    bias_two = 1.0 - beta_two**adam_step
    projected_gradient = clip_factor * projected
    new_first = beta_one * first_moment + (1.0 - beta_one) * projected_gradient
    new_second = (
        beta_two * second_moment + (1.0 - beta_two) * projected_gradient * projected_gradient
    )
    direction = new_first / bias_one / (jnp.sqrt(new_second / bias_two) + adam_eps)
    row_count = weights.shape[1]
    slab = lax.dynamic_slice_in_dim(new_bases, z * row_count, row_count, 1)
    delta = lax.dot_general(
        slab,
        direction,
        (((2,), (1,)), ((0,), (0,))),
        precision=lax.Precision.HIGH,
        preferred_element_type=jnp.float32,
    )
    delta = lax.all_gather(delta, "shard", axis=2, tiled=True)
    new_weights = weights - learn_rate * galore_scale * delta
    clipped_gain = clip_factor * gain_total
    gain_first_new = beta_one * gain_first + (1.0 - beta_one) * clipped_gain
    gain_second_new = beta_two * gain_second + (1.0 - beta_two) * clipped_gain * clipped_gain
    gain_new = gain - learn_rate * (gain_first_new / bias_one) / (
        jnp.sqrt(gain_second_new / bias_two) + adam_eps
    )
    return (
        new_weights,
        new_bases,
        new_first,
        new_second,
        gain_new,
        gain_first_new,
        gain_second_new,
    )


def solution(mesh):
    placed = (
        P(None, "dp", "tensor"),
        P("dp", None, None, ("tensor", "shard")),
        P(),
        P(None, None, ("tensor", "shard")),
        P(None, None, ("tensor", "shard")),
        P(),
        P("dp", None),
        P(),
        P(),
    )
    return jax.shard_map(
        functools.partial(per_device, mesh.shape["dp"]),
        mesh=mesh,
        in_specs=placed,
        out_specs=(
            P(None, "dp", "tensor"),
            P(),
            P(None, None, ("tensor", "shard")),
            P(None, None, ("tensor", "shard")),
            P(),
            P(),
            P(),
        ),
        check_vma=False,
    )
```

```python
import functools
import math

import jax
import jax.numpy as jnp
from jax import lax
from jax.experimental import pallas as pl
from jax.experimental.pallas import tpu as pltpu
from jax.sharding import PartitionSpec as P

NS_STEPS = 5
MATS = 2

beta_one = 0.9
beta_two = 0.999
adam_eps = 1e-08
adam_step = 100
learn_rate = 0.02
galore_scale = 0.25
norm_eps = 1e-06

MESH = pl.DeviceIdType.MESH
VMEM = pl.BlockSpec(memory_space=pltpu.VMEM)
SKEW = 2


def dot(left, right, dims, precision=lax.Precision.HIGH):
    return lax.dot_general(
        left, right, (dims, ((), ())), precision=precision, preferred_element_type=jnp.float32
    )


def greet_line(dp, z):
    barrier = pltpu.get_barrier_semaphore()
    for k in range(1, dp):
        pl.semaphore_signal(
            barrier, inc=1, device_id={"dp": lax.rem(z + k, dp)}, device_id_type=MESH
        )
    pl.semaphore_wait(barrier, dp - 1)


def chunk_rows(rows, want):
    best = 8
    for size in range(8, want + 1, 8):
        if rows % size == 0:
            best = size
    return best


def line_sum_kernel(
    dp, ch, g_ref, gain_ref, out_ref, gain_out, rbuf, gbuf, send, recv, gsend, grecv
):
    z = lax.axis_index("dp")
    nch = g_ref.shape[1] // ch
    greet_line(dp, z)

    def remote(m, c, src, target):
        rows = pl.ds(c * ch, ch)
        return pltpu.make_async_remote_copy(
            src_ref=src.at[m, rows],
            dst_ref=rbuf.at[m, rows],
            send_sem=send.at[m, c],
            recv_sem=recv.at[m, c],
            device_id={"dp": target},
            device_id_type=MESH,
        )

    hops = (dp - 1 - z, z)
    target = (jnp.maximum(z - 1, 0), jnp.minimum(z + 1, dp - 1))

    def step(i, carry):
        for m in range(MATS):
            c = i - SKEW * hops[m]
            live = jnp.logical_and(c >= 0, c < nch)
            rows = pl.ds(pl.multiple_of(c * ch, 8), ch)

            @pl.when(jnp.logical_and(live, hops[m] == 0))
            def _():
                remote(m, c, g_ref, target[m]).start()

            @pl.when(jnp.logical_and(live, hops[m] > 0))
            def _():
                remote(m, c, rbuf, target[m]).wait_recv()

            @pl.when(jnp.logical_and(live, jnp.logical_and(hops[m] > 0, hops[m] < dp - 1)))
            def _():
                rbuf[m, rows, :] = rbuf[m, rows, :] + g_ref[m, rows, :]
                remote(m, c, rbuf, target[m]).start()

            @pl.when(jnp.logical_and(live, hops[m] == dp - 1))
            def _():
                out_ref[rows, :] = rbuf[m, rows, :] + g_ref[m, rows, :]

        return carry

    gcopies = []
    for k in range(1, dp):
        copy = pltpu.make_async_remote_copy(
            src_ref=gain_ref,
            dst_ref=gbuf.at[z],
            send_sem=gsend.at[k],
            recv_sem=grecv.at[k],
            device_id={"dp": lax.rem(z + k, dp)},
            device_id_type=MESH,
        )
        copy.start()
        gcopies.append(copy)

    lax.fori_loop(0, nch + SKEW * (dp - 1), step, 0)

    for copy in gcopies:
        copy.wait()
    gbuf[pl.ds(z, 1)] = gain_ref[...][None]
    gain_out[...] = jnp.sum(gbuf[...], axis=0)

    @pl.when(jnp.logical_and(z > 0, z < dp - 1))
    def _():
        out_ref[...] = jnp.zeros_like(out_ref)

    def drain(c, carry):
        for m in range(MATS):

            @pl.when(hops[m] < dp - 1)
            def _():
                remote(m, c, rbuf, target[m]).wait_send()

        return carry

    lax.fori_loop(0, nch, drain, 0)


def line_sum(dp, grads, gain_grad):
    mats, rows, cols = grads.shape
    ch = chunk_rows(rows, 32)
    nch = rows // ch
    dma = pltpu.SemaphoreType.DMA
    return pl.pallas_call(
        functools.partial(line_sum_kernel, dp, ch),
        out_shape=(
            jax.ShapeDtypeStruct((rows, cols), jnp.float32),
            jax.ShapeDtypeStruct(gain_grad.shape, jnp.float32),
        ),
        in_specs=[VMEM, VMEM],
        out_specs=(VMEM, VMEM),
        scratch_shapes=[
            pltpu.VMEM((mats, rows, cols), jnp.float32),
            pltpu.VMEM((dp,) + gain_grad.shape, jnp.float32),
            dma((mats, nch)),
            dma((mats, nch)),
            dma((dp,)),
            dma((dp,)),
        ],
        compiler_params=pltpu.CompilerParams(
            collective_id=0, has_side_effects=True, vmem_limit_bytes=40 * 2**20
        ),
    )(grads, gain_grad)


def line_spread_kernel(dp, parts, *refs):
    n = len(parts)
    ins, outs = refs[:n], refs[n : 2 * n]
    send, recv, keep, pair_send, pair_recv = refs[2 * n :]
    z, core = lax.axis_index("dp"), lax.axis_index("tensor")
    barrier = pltpu.get_barrier_semaphore()
    for k in range(1, dp):
        pl.semaphore_signal(
            barrier, inc=1, device_id={"dp": lax.rem(z + k, dp)}, device_id_type=MESH
        )
    pl.semaphore_signal(barrier, inc=1, device_id={"tensor": 1 - core}, device_id_type=MESH)
    pl.semaphore_wait(barrier, dp)
    hops = (z, dp - 1 - z)
    target = (jnp.minimum(z + 1, dp - 1), jnp.maximum(z - 1, 0))
    plan = []
    for a, (rows, ch) in enumerate(parts):
        span = rows // 2 if a == n - 1 else rows
        plan += [(a, r, ch, span) for r in range(0, span, ch)]

    def rows_of(k, owner):
        a, r, ch, span = plan[k]
        if a < n - 1:
            return pl.ds(r, ch)
        return pl.ds(pl.multiple_of(owner * span + r, 8), ch)

    def remote(m, k, first):
        a = plan[k][0]
        rows = rows_of(k, core)
        dst = outs[a].at[m, rows]
        return pltpu.make_async_remote_copy(
            src_ref=ins[a].at[rows] if first else dst,
            dst_ref=dst,
            send_sem=send.at[m, k],
            recv_sem=recv.at[m, k],
            device_id={"dp": target[m]},
            device_id_type=MESH,
        )

    def across(m, k, owner):
        ref = outs[n - 1].at[m, rows_of(k, owner)]
        return pltpu.make_async_remote_copy(
            src_ref=ref,
            dst_ref=ref,
            send_sem=pair_send.at[m, k],
            recv_sem=pair_recv.at[m, k],
            device_id={"tensor": 1 - core},
            device_id_type=MESH,
        )

    split = [k for k in range(len(plan)) if plan[k][0] == n - 1]
    for m in range(MATS):

        @pl.when(hops[m] == 0)
        def _():
            for k in range(len(plan)):
                remote(m, k, True).start()
            for a in range(n):
                pltpu.make_async_copy(ins[a], outs[a].at[m], keep.at[a]).start()

    for i in range(len(plan) + SKEW * (dp - 1)):
        for m in range(MATS):
            for h in range(1, dp):
                k = i - SKEW * h
                if 0 <= k < len(plan):

                    @pl.when(hops[m] == h)
                    def _():
                        remote(m, k, False).wait_recv()
                        if h < dp - 1:
                            remote(m, k, False).start()
                        if k in split:
                            across(m, k, core).start()

    for m in range(MATS):

        @pl.when(hops[m] == 0)
        def _():
            for a in range(n):
                pltpu.make_async_copy(ins[a], outs[a].at[m], keep.at[a]).wait()

        @pl.when(hops[m] > 0)
        def _():
            for k in split:
                across(m, k, core).wait_send()
                across(m, k, 1 - core).wait_recv()

        @pl.when(hops[m] < dp - 1)
        def _():
            for k in range(len(plan)):
                remote(m, k, False).wait_send()


def line_spread(dp, arrays, sizes):
    parts = tuple((a.shape[0], size) for a, size in zip(arrays, sizes))
    nk = sum(a.shape[0] // size for a, size in zip(arrays, sizes))
    dma = pltpu.SemaphoreType.DMA
    return pl.pallas_call(
        functools.partial(line_spread_kernel, dp, parts),
        out_shape=tuple(jax.ShapeDtypeStruct((MATS,) + a.shape, jnp.float32) for a in arrays),
        in_specs=[VMEM] * len(arrays),
        out_specs=tuple(VMEM for _ in arrays),
        scratch_shapes=[dma((MATS, nk))] * 2 + [dma((len(arrays),))] + [dma((MATS, nk))] * 2,
        compiler_params=pltpu.CompilerParams(
            collective_id=1, has_side_effects=True, vmem_limit_bytes=32 * 2**20
        ),
    )(*arrays)


def plane_sum_kernel(
    x_ref, sq_ref, out_ref, sq_out, abuf, hbuf, bbuf, sqbuf, a_sem, b_sem, c_sem, d_sem, s_sem
):
    core, s = lax.axis_index("tensor"), lax.axis_index("shard")
    half = x_ref.shape[0] // 2
    piece = half // 4
    barrier = pltpu.get_barrier_semaphore()
    others = [(lax.rem(core + i, 2), lax.rem(s + k, 4)) for i in range(2) for k in range(4)][1:]
    for c, t in others:
        pl.semaphore_signal(
            barrier, inc=1, device_id={"tensor": c, "shard": t}, device_id_type=MESH
        )
    pl.semaphore_wait(barrier, 7)

    def remote(src, dst, sems, i, device):
        return pltpu.make_async_remote_copy(
            src_ref=src,
            dst_ref=dst,
            send_sem=sems.at[0, i],
            recv_sem=sems.at[1, i],
            device_id=device,
            device_id_type=MESH,
        )

    def rows_at(start):
        return pl.ds(pl.multiple_of(start, 8), piece)

    sibling = {"tensor": 1 - core}
    order = [lax.rem(s + k, 4) for k in (1, 2, 3, 0)]
    pair = []
    for i, t in enumerate(order):
        rows = rows_at(t * piece)
        copy = remote(
            x_ref.at[rows_at((1 - core) * half + t * piece)], abuf.at[rows], a_sem, i, sibling
        )
        copy.start()
        pair.append(copy)
    me = core * 4 + s
    squares = []
    for i, (c, t) in enumerate(others):
        copy = remote(sq_ref, sqbuf.at[me], s_sem, i, {"tensor": c, "shard": t})
        copy.start()
        squares.append(copy)
    spread = []
    for i, t in enumerate(order):
        rows = rows_at(t * piece)
        pair[i].wait_recv()
        hbuf[rows, :] = x_ref[rows_at(core * half + t * piece), :] + abuf[rows, :]
        if i < 3:
            copy = remote(hbuf.at[rows], bbuf.at[i], b_sem, i, {"shard": t})
            copy.start()
            spread.append(copy)
    mine = rows_at(core * half + s * piece)
    for copy in spread:
        copy.wait_recv()
    out_ref[mine, :] = (hbuf[rows_at(s * piece), :] + bbuf[0]) + (bbuf[1] + bbuf[2])
    gather = []
    for i in range(3):
        copy = remote(out_ref.at[mine], out_ref.at[mine], c_sem, i, {"shard": order[i]})
        copy.start()
        gather.append(copy)
    across = [remote(out_ref.at[mine], out_ref.at[mine], d_sem, 3, sibling)]
    across[0].start()
    for i in range(3):
        gather[i].wait_recv()
        rows = rows_at(core * half + lax.rem(s + 3 - i, 4) * piece)
        copy = remote(out_ref.at[rows], out_ref.at[rows], d_sem, i, sibling)
        copy.start()
        across.append(copy)
    for copy in squares:
        copy.wait()
    sqbuf[pl.ds(me, 1)] = sq_ref[...][None]
    sq_out[...] = jnp.sum(sqbuf[...], axis=0)
    for copy in across:
        copy.wait()
    for copy in pair + spread + gather:
        copy.wait_send()


def plane_sum(partial, squares):
    rows, rank = partial.shape
    piece = rows // 8
    dma = pltpu.SemaphoreType.DMA
    return pl.pallas_call(
        plane_sum_kernel,
        out_shape=(
            jax.ShapeDtypeStruct(partial.shape, jnp.float32),
            jax.ShapeDtypeStruct(squares.shape, jnp.float32),
        ),
        in_specs=[VMEM, VMEM],
        out_specs=(VMEM, VMEM),
        scratch_shapes=[
            pltpu.VMEM((rows // 2, rank), jnp.float32),
            pltpu.VMEM((rows // 2, rank), jnp.float32),
            pltpu.VMEM((3, piece, rank), jnp.float32),
            pltpu.VMEM((8,) + squares.shape, jnp.float32),
            dma((2, 4)),
            dma((2, 3)),
            dma((2, 3)),
            dma((2, 4)),
            dma((2, 7)),
        ],
        compiler_params=pltpu.CompilerParams(collective_id=2, has_side_effects=True),
    )(partial, squares)


def gather_kernel(ch, rate, delta_ref, w_ref, out_ref, rbuf, own_sem, fwd_sem, recv_sem):
    s = lax.axis_index("shard")
    y, x = s // 2, lax.rem(s, 2)
    source = (y * 2 + (1 - x), (1 - y) * 2 + x, (1 - y) * 2 + (1 - x))
    barrier = pltpu.get_barrier_semaphore()
    for r in range(2):
        pl.semaphore_signal(barrier, inc=1, device_id={"shard": source[r]}, device_id_type=MESH)
    pl.semaphore_wait(barrier, 2)
    mats, rows, cols = delta_ref.shape
    per = rows // ch
    nch = mats * per

    def place(ref, j):
        return ref.at[j // per, pl.ds(pl.multiple_of(lax.rem(j, per) * ch, 8), ch)]

    def own(r, j):
        return pltpu.make_async_remote_copy(
            src_ref=place(delta_ref, j),
            dst_ref=place(rbuf.at[r], j),
            send_sem=own_sem.at[r, j],
            recv_sem=recv_sem.at[r, j],
            device_id={"shard": source[r]},
            device_id_type=MESH,
        )

    def forward(r, j):
        return pltpu.make_async_remote_copy(
            src_ref=place(rbuf.at[1 - r], j),
            dst_ref=place(rbuf.at[2], j),
            send_sem=fwd_sem.at[j],
            recv_sem=recv_sem.at[2, j],
            device_id={"shard": source[r]},
            device_id_type=MESH,
        )

    def start(j, carry):
        for r in range(2):
            own(r, j).start()
        return carry

    lax.fori_loop(0, nch, start, 0)

    def write(j, src, chunk):
        m = j // per
        at = pl.ds(pl.multiple_of(lax.rem(j, per) * ch, 8), ch)
        for t in range(4):

            @pl.when(src == t)
            def _():
                lanes = slice(t * cols, (t + 1) * cols)
                out_ref[m, at, lanes] = w_ref[m, at, lanes] - rate * chunk[...]

    def near(j, carry):
        for r in range(2):
            own(r, j).wait_recv()
        for r in range(2):

            @pl.when(lax.rem(j, 2) == r)
            def _():
                forward(r, j).start()

        write(j, s, place(delta_ref, j))
        for r in range(2):
            write(j, source[r], place(rbuf.at[r], j))
        return carry

    lax.fori_loop(0, nch, near, 0)

    def far(j, carry):
        forward(0, j).wait()
        write(j, source[2], place(rbuf.at[2], j))
        for r in range(2):
            own(r, j).wait_send()
        return carry

    lax.fori_loop(0, nch, far, 0)


def gather_update(delta, weights, rate):
    mats, rows, cols = delta.shape
    ch = chunk_rows(rows, 56)
    nch = mats * (rows // ch)
    dma = pltpu.SemaphoreType.DMA
    return pl.pallas_call(
        functools.partial(gather_kernel, ch, rate),
        out_shape=jax.ShapeDtypeStruct(weights.shape, jnp.float32),
        in_specs=[VMEM, VMEM],
        out_specs=VMEM,
        scratch_shapes=[
            pltpu.VMEM((3, mats, rows, cols), jnp.float32),
            dma((2, nch)),
            dma((nch,)),
            dma((3, nch)),
        ],
        compiler_params=pltpu.CompilerParams(
            collective_id=3, has_side_effects=True, vmem_limit_bytes=40 * 2**20
        ),
    )(delta, weights)


def per_device(
    dp,
    weights,
    grads,
    bases,
    first_moment,
    second_moment,
    gain,
    gain_grad,
    gain_first,
    gain_second,
):
    z = lax.axis_index("dp")
    shards = lax.axis_size("shard")
    ff = first_moment.shape[2] * lax.axis_size("tensor") * shards
    mine, gain_total = line_sum(dp, jnp.swapaxes(grads[0], 1, 2), gain_grad)
    gain_total = gain_total[0]
    basis = lax.dynamic_index_in_dim(bases, jnp.where(z * 2 >= dp, 1, 0), 0, keepdims=False)
    rows, rank = basis.shape
    squares = jnp.full((8, 128), jnp.sum(mine * mine), jnp.float32)
    carried = dot(mine, basis, ((1,), (0,)))
    partial = dot(mine, carried, ((0,), (0,)))
    direct = shards == 4 and lax.axis_size("tensor") == 2 and rows % 64 == 0
    if direct:
        sketch, squares = plane_sum(partial, squares)
    else:
        sketch, squares = lax.psum((partial, squares), ("tensor", "shard"))
    iterate = sketch / (jnp.sqrt(jnp.sum(sketch * sketch)) + norm_eps)
    gram = dot(iterate, iterate, ((0,), (0,)))
    eye = jnp.eye(rank, dtype=jnp.float32)
    product = None
    for turn in range(NS_STEPS):
        factor = 1.5 * eye - 0.5 * gram
        product = factor if product is None else dot(product, factor, ((1,), (0,)))
        if turn < NS_STEPS - 1:
            gram = dot(dot(factor, gram, ((1,), (0,))), factor, ((1,), (0,)))
    new_basis = dot(iterate, product, ((1,), (0,)))
    projected = dot(mine, new_basis, ((1,), (0,)))
    projected, squares, new_bases = line_spread(
        dp,
        (projected, squares, new_basis),
        (chunk_rows(projected.shape[0], 32), 8, chunk_rows(rows // 2, 64)),
    )

    total_squares = squares[0, 0, 0] + squares[1, 0, 0] + jnp.sum(gain_total * gain_total)
    clip_factor = jnp.minimum(1.0, math.sqrt(MATS * ff) / (jnp.sqrt(total_squares) + norm_eps))
    bias_one = 1.0 - beta_one**adam_step
    bias_two = 1.0 - beta_two**adam_step
    projected_gradient = clip_factor * projected
    new_first = beta_one * jnp.swapaxes(first_moment, 1, 2) + (1.0 - beta_one) * projected_gradient
    new_second = (
        beta_two * jnp.swapaxes(second_moment, 1, 2)
        + (1.0 - beta_two) * projected_gradient * projected_gradient
    )
    direction = new_first / bias_one / (jnp.sqrt(new_second / bias_two) + adam_eps)
    new_first, new_second = jnp.swapaxes(new_first, 1, 2), jnp.swapaxes(new_second, 1, 2)
    row_count = weights.shape[1]
    slab = lax.dynamic_slice_in_dim(new_bases, z * row_count, row_count, 1)
    delta = lax.dot_general(
        slab,
        direction,
        (((2,), (2,)), ((0,), (0,))),
        precision=lax.Precision.HIGH,
        preferred_element_type=jnp.float32,
    )
    if direct:
        new_weights = gather_update(delta, weights, learn_rate * galore_scale)
    else:
        delta = lax.all_gather(delta, "shard", axis=2, tiled=True)
        new_weights = weights - learn_rate * galore_scale * delta
    clipped_gain = clip_factor * gain_total
    gain_first_new = beta_one * gain_first + (1.0 - beta_one) * clipped_gain
    gain_second_new = beta_two * gain_second + (1.0 - beta_two) * clipped_gain * clipped_gain
    gain_new = gain - learn_rate * (gain_first_new / bias_one) / (
        jnp.sqrt(gain_second_new / bias_two) + adam_eps
    )
    return (
        new_weights,
        new_bases,
        new_first,
        new_second,
        gain_new,
        gain_first_new,
        gain_second_new,
    )


def solution(mesh):
    placed = (
        P(None, "dp", "tensor"),
        P("dp", None, None, ("tensor", "shard")),
        P(),
        P(None, None, ("tensor", "shard")),
        P(None, None, ("tensor", "shard")),
        P(),
        P("dp", None),
        P(),
        P(),
    )
    return jax.shard_map(
        functools.partial(per_device, mesh.shape["dp"]),
        mesh=mesh,
        in_specs=placed,
        out_specs=(
            P(None, "dp", "tensor"),
            P(),
            P(None, None, ("tensor", "shard")),
            P(None, None, ("tensor", "shard")),
            P(),
            P(),
            P(),
        ),
        check_vma=False,
    )
```

```python
import functools
import math

import jax
import jax.numpy as jnp
from jax import lax
from jax.experimental import pallas as pl
from jax.experimental.pallas import tpu as pltpu
from jax.sharding import PartitionSpec as P

NS_STEPS = 5
MATS = 2

beta_one = 0.9
beta_two = 0.999
adam_eps = 1e-08
adam_step = 100
learn_rate = 0.02
galore_scale = 0.25
norm_eps = 1e-06

MESH = pl.DeviceIdType.MESH
VMEM = pl.BlockSpec(memory_space=pltpu.VMEM)
SUM_SKEW = 4
SPREAD_SKEW = 8


def dot(left, right, dims, precision=lax.Precision.HIGH):
    return lax.dot_general(
        left, right, (dims, ((), ())), precision=precision, preferred_element_type=jnp.float32
    )


def greet_line(dp, z):
    barrier = pltpu.get_barrier_semaphore()
    for k in range(1, dp):
        pl.semaphore_signal(
            barrier, inc=1, device_id={"dp": lax.rem(z + k, dp)}, device_id_type=MESH
        )
    pl.semaphore_wait(barrier, dp - 1)


def chunk_rows(rows, want):
    best = 8
    for size in range(8, want + 1, 8):
        if rows % size == 0:
            best = size
    return best


def line_sum_kernel(
    dp, ch, g_ref, gain_ref, out_ref, gain_out, rbuf, gbuf, send, recv, gsend, grecv
):
    z = lax.axis_index("dp")
    nch = g_ref.shape[1] // ch
    greet_line(dp, z)

    def remote(m, c, src, target):
        rows = pl.ds(c * ch, ch)
        return pltpu.make_async_remote_copy(
            src_ref=src.at[m, rows],
            dst_ref=rbuf.at[m, rows],
            send_sem=send.at[m, c],
            recv_sem=recv.at[m, c],
            device_id={"dp": target},
            device_id_type=MESH,
        )

    hops = (dp - 1 - z, z)
    target = (jnp.maximum(z - 1, 0), jnp.minimum(z + 1, dp - 1))

    def step(i, carry):
        for m in range(MATS):
            c = i - SUM_SKEW * hops[m]
            live = jnp.logical_and(c >= 0, c < nch)
            rows = pl.ds(pl.multiple_of(c * ch, 8), ch)

            @pl.when(jnp.logical_and(live, hops[m] == 0))
            def _():
                remote(m, c, g_ref, target[m]).start()

            @pl.when(jnp.logical_and(live, hops[m] > 0))
            def _():
                remote(m, c, rbuf, target[m]).wait_recv()

            @pl.when(jnp.logical_and(live, jnp.logical_and(hops[m] > 0, hops[m] < dp - 1)))
            def _():
                rbuf[m, rows, :] = rbuf[m, rows, :] + g_ref[m, rows, :]
                remote(m, c, rbuf, target[m]).start()

            @pl.when(jnp.logical_and(live, hops[m] == dp - 1))
            def _():
                out_ref[rows, :] = rbuf[m, rows, :] + g_ref[m, rows, :]

        return carry

    gcopies = []
    for k in range(1, dp):
        copy = pltpu.make_async_remote_copy(
            src_ref=gain_ref,
            dst_ref=gbuf.at[z],
            send_sem=gsend.at[k],
            recv_sem=grecv.at[k],
            device_id={"dp": lax.rem(z + k, dp)},
            device_id_type=MESH,
        )
        copy.start()
        gcopies.append(copy)

    lax.fori_loop(0, nch + SUM_SKEW * (dp - 1), step, 0)

    for copy in gcopies:
        copy.wait()
    gbuf[pl.ds(z, 1)] = gain_ref[...][None]
    gain_out[...] = jnp.sum(gbuf[...], axis=0)

    @pl.when(jnp.logical_and(z > 0, z < dp - 1))
    def _():
        out_ref[...] = jnp.zeros_like(out_ref)

    def drain(c, carry):
        for m in range(MATS):

            @pl.when(hops[m] < dp - 1)
            def _():
                remote(m, c, rbuf, target[m]).wait_send()

        return carry

    lax.fori_loop(0, nch, drain, 0)


def line_sum(dp, grads, gain_grad):
    mats, rows, cols = grads.shape
    ch = chunk_rows(rows, 16)
    nch = rows // ch
    dma = pltpu.SemaphoreType.DMA
    return pl.pallas_call(
        functools.partial(line_sum_kernel, dp, ch),
        out_shape=(
            jax.ShapeDtypeStruct((rows, cols), jnp.float32),
            jax.ShapeDtypeStruct(gain_grad.shape, jnp.float32),
        ),
        in_specs=[VMEM, VMEM],
        out_specs=(VMEM, VMEM),
        scratch_shapes=[
            pltpu.VMEM((mats, rows, cols), jnp.float32),
            pltpu.VMEM((dp,) + gain_grad.shape, jnp.float32),
            dma((mats, nch)),
            dma((mats, nch)),
            dma((dp,)),
            dma((dp,)),
        ],
        compiler_params=pltpu.CompilerParams(
            collective_id=0, has_side_effects=True, vmem_limit_bytes=40 * 2**20
        ),
    )(grads, gain_grad)


def line_spread_kernel(dp, parts, *refs):
    n = len(parts)
    ins, outs = refs[:n], refs[n : 2 * n]
    send, recv, keep, pair_send, pair_recv = refs[2 * n :]
    z, core = lax.axis_index("dp"), lax.axis_index("tensor")
    barrier = pltpu.get_barrier_semaphore()
    for k in range(1, dp):
        pl.semaphore_signal(
            barrier, inc=1, device_id={"dp": lax.rem(z + k, dp)}, device_id_type=MESH
        )
    pl.semaphore_signal(barrier, inc=1, device_id={"tensor": 1 - core}, device_id_type=MESH)
    pl.semaphore_wait(barrier, dp)
    hops = (z, dp - 1 - z)
    target = (jnp.minimum(z + 1, dp - 1), jnp.maximum(z - 1, 0))
    plan = []
    for a, (rows, ch) in enumerate(parts):
        span = rows // 2 if a == n - 1 else rows
        plan += [(a, r, ch, span) for r in range(0, span, ch)]

    def rows_of(k, owner):
        a, r, ch, span = plan[k]
        if a < n - 1:
            return pl.ds(r, ch)
        return pl.ds(pl.multiple_of(owner * span + r, 8), ch)

    def remote(m, k, first):
        a = plan[k][0]
        rows = rows_of(k, core)
        dst = outs[a].at[m, rows]
        return pltpu.make_async_remote_copy(
            src_ref=ins[a].at[rows] if first else dst,
            dst_ref=dst,
            send_sem=send.at[m, k],
            recv_sem=recv.at[m, k],
            device_id={"dp": target[m]},
            device_id_type=MESH,
        )

    def across(m, k, owner):
        ref = outs[n - 1].at[m, rows_of(k, owner)]
        return pltpu.make_async_remote_copy(
            src_ref=ref,
            dst_ref=ref,
            send_sem=pair_send.at[m, k],
            recv_sem=pair_recv.at[m, k],
            device_id={"tensor": 1 - core},
            device_id_type=MESH,
        )

    split = [k for k in range(len(plan)) if plan[k][0] == n - 1]
    for m in range(MATS):

        @pl.when(hops[m] == 0)
        def _():
            for k in range(len(plan)):
                remote(m, k, True).start()
            for a in range(n):
                pltpu.make_async_copy(ins[a], outs[a].at[m], keep.at[a]).start()

    for i in range(len(plan) + SPREAD_SKEW * (dp - 1)):
        for m in range(MATS):
            for h in range(1, dp):
                k = i - SPREAD_SKEW * h
                if 0 <= k < len(plan):

                    @pl.when(hops[m] == h)
                    def _():
                        remote(m, k, False).wait_recv()
                        if h < dp - 1:
                            remote(m, k, False).start()
                        if k in split:
                            across(m, k, core).start()

    for m in range(MATS):

        @pl.when(hops[m] == 0)
        def _():
            for a in range(n):
                pltpu.make_async_copy(ins[a], outs[a].at[m], keep.at[a]).wait()

        @pl.when(hops[m] > 0)
        def _():
            for k in split:
                across(m, k, core).wait_send()
                across(m, k, 1 - core).wait_recv()

        @pl.when(hops[m] < dp - 1)
        def _():
            for k in range(len(plan)):
                remote(m, k, False).wait_send()


def line_spread(dp, arrays, sizes):
    parts = tuple((a.shape[0], size) for a, size in zip(arrays, sizes))
    nk = sum(a.shape[0] // size for a, size in zip(arrays, sizes))
    dma = pltpu.SemaphoreType.DMA
    return pl.pallas_call(
        functools.partial(line_spread_kernel, dp, parts),
        out_shape=tuple(jax.ShapeDtypeStruct((MATS,) + a.shape, jnp.float32) for a in arrays),
        in_specs=[VMEM] * len(arrays),
        out_specs=tuple(VMEM for _ in arrays),
        scratch_shapes=[dma((MATS, nk))] * 2 + [dma((len(arrays),))] + [dma((MATS, nk))] * 2,
        compiler_params=pltpu.CompilerParams(
            collective_id=1, has_side_effects=True, vmem_limit_bytes=32 * 2**20
        ),
    )(*arrays)


def plane_sum_kernel(
    x_ref, sq_ref, out_ref, sq_out, abuf, hbuf, bbuf, sqbuf, a_sem, b_sem, c_sem, d_sem, s_sem
):
    core, s = lax.axis_index("tensor"), lax.axis_index("shard")
    half = x_ref.shape[0] // 2
    piece = half // 4
    barrier = pltpu.get_barrier_semaphore()
    others = [(lax.rem(core + i, 2), lax.rem(s + k, 4)) for i in range(2) for k in range(4)][1:]
    for c, t in others:
        pl.semaphore_signal(
            barrier, inc=1, device_id={"tensor": c, "shard": t}, device_id_type=MESH
        )
    pl.semaphore_wait(barrier, 7)

    def remote(src, dst, sems, i, device):
        return pltpu.make_async_remote_copy(
            src_ref=src,
            dst_ref=dst,
            send_sem=sems.at[0, i],
            recv_sem=sems.at[1, i],
            device_id=device,
            device_id_type=MESH,
        )

    def rows_at(start):
        return pl.ds(pl.multiple_of(start, 8), piece)

    sibling = {"tensor": 1 - core}
    order = [lax.rem(s + k, 4) for k in (1, 2, 3, 0)]
    pair = []
    for i, t in enumerate(order):
        rows = rows_at(t * piece)
        copy = remote(
            x_ref.at[rows_at((1 - core) * half + t * piece)], abuf.at[rows], a_sem, i, sibling
        )
        copy.start()
        pair.append(copy)
    me = core * 4 + s
    squares = []
    for i, (c, t) in enumerate(others):
        copy = remote(sq_ref, sqbuf.at[me], s_sem, i, {"tensor": c, "shard": t})
        copy.start()
        squares.append(copy)
    spread = []
    for i, t in enumerate(order):
        rows = rows_at(t * piece)
        pair[i].wait_recv()
        hbuf[rows, :] = x_ref[rows_at(core * half + t * piece), :] + abuf[rows, :]
        if i < 3:
            copy = remote(hbuf.at[rows], bbuf.at[i], b_sem, i, {"shard": t})
            copy.start()
            spread.append(copy)
    mine = rows_at(core * half + s * piece)
    for copy in spread:
        copy.wait_recv()
    out_ref[mine, :] = (hbuf[rows_at(s * piece), :] + bbuf[0]) + (bbuf[1] + bbuf[2])
    gather = []
    for i in range(3):
        copy = remote(out_ref.at[mine], out_ref.at[mine], c_sem, i, {"shard": order[i]})
        copy.start()
        gather.append(copy)
    across = [remote(out_ref.at[mine], out_ref.at[mine], d_sem, 3, sibling)]
    across[0].start()
    for i in range(3):
        gather[i].wait_recv()
        rows = rows_at(core * half + lax.rem(s + 3 - i, 4) * piece)
        copy = remote(out_ref.at[rows], out_ref.at[rows], d_sem, i, sibling)
        copy.start()
        across.append(copy)
    for copy in squares:
        copy.wait()
    sqbuf[pl.ds(me, 1)] = sq_ref[...][None]
    sq_out[...] = jnp.sum(sqbuf[...], axis=0)
    for copy in across:
        copy.wait()
    for copy in pair + spread + gather:
        copy.wait_send()


def plane_sum(partial, squares):
    rows, rank = partial.shape
    piece = rows // 8
    dma = pltpu.SemaphoreType.DMA
    return pl.pallas_call(
        plane_sum_kernel,
        out_shape=(
            jax.ShapeDtypeStruct(partial.shape, jnp.float32),
            jax.ShapeDtypeStruct(squares.shape, jnp.float32),
        ),
        in_specs=[VMEM, VMEM],
        out_specs=(VMEM, VMEM),
        scratch_shapes=[
            pltpu.VMEM((rows // 2, rank), jnp.float32),
            pltpu.VMEM((rows // 2, rank), jnp.float32),
            pltpu.VMEM((3, piece, rank), jnp.float32),
            pltpu.VMEM((8,) + squares.shape, jnp.float32),
            dma((2, 4)),
            dma((2, 3)),
            dma((2, 3)),
            dma((2, 4)),
            dma((2, 7)),
        ],
        compiler_params=pltpu.CompilerParams(collective_id=2, has_side_effects=True),
    )(partial, squares)


def gather_kernel(ch, rate, delta_ref, w_ref, out_ref, rbuf, own_sem, fwd_sem, recv_sem):
    s = lax.axis_index("shard")
    y, x = s // 2, lax.rem(s, 2)
    source = (y * 2 + (1 - x), (1 - y) * 2 + x, (1 - y) * 2 + (1 - x))
    barrier = pltpu.get_barrier_semaphore()
    for r in range(2):
        pl.semaphore_signal(barrier, inc=1, device_id={"shard": source[r]}, device_id_type=MESH)
    pl.semaphore_wait(barrier, 2)
    mats, rows, cols = delta_ref.shape
    per = rows // ch
    nch = mats * per

    def place(ref, j):
        return ref.at[j // per, pl.ds(pl.multiple_of(lax.rem(j, per) * ch, 8), ch)]

    def own(r, j):
        return pltpu.make_async_remote_copy(
            src_ref=place(delta_ref, j),
            dst_ref=place(rbuf.at[r], j),
            send_sem=own_sem.at[r, j],
            recv_sem=recv_sem.at[r, j],
            device_id={"shard": source[r]},
            device_id_type=MESH,
        )

    def forward(r, j):
        return pltpu.make_async_remote_copy(
            src_ref=place(rbuf.at[1 - r], j),
            dst_ref=place(rbuf.at[2], j),
            send_sem=fwd_sem.at[j],
            recv_sem=recv_sem.at[2, j],
            device_id={"shard": source[r]},
            device_id_type=MESH,
        )

    def start(j, carry):
        for r in range(2):
            own(r, j).start()
        return carry

    lax.fori_loop(0, nch, start, 0)

    def write(j, src, chunk):
        m = j // per
        at = pl.ds(pl.multiple_of(lax.rem(j, per) * ch, 8), ch)
        for t in range(4):

            @pl.when(src == t)
            def _():
                lanes = slice(t * cols, (t + 1) * cols)
                out_ref[m, at, lanes] = w_ref[m, at, lanes] - rate * chunk[...]

    def near(j, carry):
        for r in range(2):
            own(r, j).wait_recv()
        for r in range(2):

            @pl.when(lax.rem(j, 2) == r)
            def _():
                forward(r, j).start()

        write(j, s, place(delta_ref, j))
        for r in range(2):
            write(j, source[r], place(rbuf.at[r], j))
        return carry

    lax.fori_loop(0, nch, near, 0)

    def far(j, carry):
        forward(0, j).wait()
        write(j, source[2], place(rbuf.at[2], j))
        for r in range(2):
            own(r, j).wait_send()
        return carry

    lax.fori_loop(0, nch, far, 0)


def gather_update(delta, weights, rate):
    mats, rows, cols = delta.shape
    ch = chunk_rows(rows, 56)
    nch = mats * (rows // ch)
    dma = pltpu.SemaphoreType.DMA
    return pl.pallas_call(
        functools.partial(gather_kernel, ch, rate),
        out_shape=jax.ShapeDtypeStruct(weights.shape, jnp.float32),
        in_specs=[VMEM, VMEM],
        out_specs=VMEM,
        scratch_shapes=[
            pltpu.VMEM((3, mats, rows, cols), jnp.float32),
            dma((2, nch)),
            dma((nch,)),
            dma((3, nch)),
        ],
        compiler_params=pltpu.CompilerParams(
            collective_id=3, has_side_effects=True, vmem_limit_bytes=40 * 2**20
        ),
    )(delta, weights)


def per_device(
    dp,
    weights,
    grads,
    bases,
    first_moment,
    second_moment,
    gain,
    gain_grad,
    gain_first,
    gain_second,
):
    z = lax.axis_index("dp")
    shards = lax.axis_size("shard")
    ff = first_moment.shape[2] * lax.axis_size("tensor") * shards
    mine, gain_total = line_sum(dp, jnp.swapaxes(grads[0], 1, 2), gain_grad)
    gain_total = gain_total[0]
    basis = lax.dynamic_index_in_dim(bases, jnp.where(z * 2 >= dp, 1, 0), 0, keepdims=False)
    rows, rank = basis.shape
    squares = jnp.full((8, 128), jnp.sum(mine * mine), jnp.float32)
    carried = dot(mine, basis, ((1,), (0,)))
    partial = dot(mine, carried, ((0,), (0,)))
    direct = shards == 4 and lax.axis_size("tensor") == 2 and rows % 64 == 0
    if direct:
        sketch, squares = plane_sum(partial, squares)
    else:
        sketch, squares = lax.psum((partial, squares), ("tensor", "shard"))
    iterate = sketch / (jnp.sqrt(jnp.sum(sketch * sketch)) + norm_eps)
    gram = dot(iterate, iterate, ((0,), (0,)))
    eye = jnp.eye(rank, dtype=jnp.float32)
    product = None
    for turn in range(NS_STEPS):
        factor = 1.5 * eye - 0.5 * gram
        product = factor if product is None else dot(product, factor, ((1,), (0,)))
        if turn < NS_STEPS - 1:
            gram = dot(dot(factor, gram, ((1,), (0,))), factor, ((1,), (0,)))
    new_basis = dot(iterate, product, ((1,), (0,)))
    projected = dot(mine, new_basis, ((1,), (0,)))
    projected, squares, new_bases = line_spread(
        dp,
        (projected, squares, new_basis),
        (chunk_rows(projected.shape[0], 32), 8, chunk_rows(rows // 2, 64)),
    )

    total_squares = squares[0, 0, 0] + squares[1, 0, 0] + jnp.sum(gain_total * gain_total)
    clip_factor = jnp.minimum(1.0, math.sqrt(MATS * ff) / (jnp.sqrt(total_squares) + norm_eps))
    bias_one = 1.0 - beta_one**adam_step
    bias_two = 1.0 - beta_two**adam_step
    projected_gradient = clip_factor * projected
    new_first = beta_one * jnp.swapaxes(first_moment, 1, 2) + (1.0 - beta_one) * projected_gradient
    new_second = (
        beta_two * jnp.swapaxes(second_moment, 1, 2)
        + (1.0 - beta_two) * projected_gradient * projected_gradient
    )
    direction = new_first / bias_one / (jnp.sqrt(new_second / bias_two) + adam_eps)
    new_first, new_second = jnp.swapaxes(new_first, 1, 2), jnp.swapaxes(new_second, 1, 2)
    row_count = weights.shape[1]
    slab = lax.dynamic_slice_in_dim(new_bases, z * row_count, row_count, 1)
    delta = lax.dot_general(
        slab,
        direction,
        (((2,), (2,)), ((0,), (0,))),
        precision=lax.Precision.HIGH,
        preferred_element_type=jnp.float32,
    )
    if direct:
        new_weights = gather_update(delta, weights, learn_rate * galore_scale)
    else:
        delta = lax.all_gather(delta, "shard", axis=2, tiled=True)
        new_weights = weights - learn_rate * galore_scale * delta
    clipped_gain = clip_factor * gain_total
    gain_first_new = beta_one * gain_first + (1.0 - beta_one) * clipped_gain
    gain_second_new = beta_two * gain_second + (1.0 - beta_two) * clipped_gain * clipped_gain
    gain_new = gain - learn_rate * (gain_first_new / bias_one) / (
        jnp.sqrt(gain_second_new / bias_two) + adam_eps
    )
    return (
        new_weights,
        new_bases,
        new_first,
        new_second,
        gain_new,
        gain_first_new,
        gain_second_new,
    )


def solution(mesh):
    placed = (
        P(None, "dp", "tensor"),
        P("dp", None, None, ("tensor", "shard")),
        P(),
        P(None, None, ("tensor", "shard")),
        P(None, None, ("tensor", "shard")),
        P(),
        P("dp", None),
        P(),
        P(),
    )
    return jax.shard_map(
        functools.partial(per_device, mesh.shape["dp"]),
        mesh=mesh,
        in_specs=placed,
        out_specs=(
            P(None, "dp", "tensor"),
            P(),
            P(None, None, ("tensor", "shard")),
            P(None, None, ("tensor", "shard")),
            P(),
            P(),
            P(),
        ),
        check_vma=False,
    )
```

```python
import functools
import math

import jax
import jax.numpy as jnp
from jax import lax
from jax.experimental import pallas as pl
from jax.experimental.pallas import tpu as pltpu
from jax.sharding import PartitionSpec as P

NS_STEPS = 5
MATS = 2

beta_one = 0.9
beta_two = 0.999
adam_eps = 1e-08
adam_step = 100
learn_rate = 0.02
galore_scale = 0.25
norm_eps = 1e-06

MESH = pl.DeviceIdType.MESH
VMEM = pl.BlockSpec(memory_space=pltpu.VMEM)
SUM_SKEW = 4
SPREAD_SKEW = 8


def dot(left, right, dims, precision=lax.Precision.HIGH):
    return lax.dot_general(
        left, right, (dims, ((), ())), precision=precision, preferred_element_type=jnp.float32
    )


def greet_line(dp, z):
    barrier = pltpu.get_barrier_semaphore()
    for k in range(1, dp):
        pl.semaphore_signal(
            barrier, inc=1, device_id={"dp": lax.rem(z + k, dp)}, device_id_type=MESH
        )
    pl.semaphore_wait(barrier, dp - 1)


def chunk_rows(rows, want):
    best = 8
    for size in range(8, want + 1, 8):
        if rows % size == 0:
            best = size
    return best


def line_sum_kernel(
    dp, ch, g_ref, gain_ref, out_ref, gain_out, sq_out, rbuf, gbuf, acc, send, recv, gsend, grecv
):
    z = lax.axis_index("dp")
    nch = g_ref.shape[1] // ch
    greet_line(dp, z)

    def remote(m, c, src, target):
        rows = pl.ds(c * ch, ch)
        return pltpu.make_async_remote_copy(
            src_ref=src.at[m, rows],
            dst_ref=rbuf.at[m, rows],
            send_sem=send.at[m, c],
            recv_sem=recv.at[m, c],
            device_id={"dp": target},
            device_id_type=MESH,
        )

    hops = (dp - 1 - z, z)
    target = (jnp.maximum(z - 1, 0), jnp.minimum(z + 1, dp - 1))

    def step(i, carry):
        for m in range(MATS):
            c = i - SUM_SKEW * hops[m]
            live = jnp.logical_and(c >= 0, c < nch)
            rows = pl.ds(pl.multiple_of(c * ch, 8), ch)

            @pl.when(jnp.logical_and(live, hops[m] == 0))
            def _():
                remote(m, c, g_ref, target[m]).start()

            @pl.when(jnp.logical_and(live, hops[m] > 0))
            def _():
                remote(m, c, rbuf, target[m]).wait_recv()

            @pl.when(jnp.logical_and(live, jnp.logical_and(hops[m] > 0, hops[m] < dp - 1)))
            def _():
                rbuf[m, rows, :] = rbuf[m, rows, :] + g_ref[m, rows, :]
                remote(m, c, rbuf, target[m]).start()

            @pl.when(jnp.logical_and(live, hops[m] == dp - 1))
            def _():
                total = rbuf[m, rows, :] + g_ref[m, rows, :]
                out_ref[rows, :] = total
                for r in range(0, ch, 8):
                    acc[...] += total[r : r + 8] * total[r : r + 8]

        return carry

    acc[...] = jnp.zeros_like(acc)
    gcopies = []
    for k in range(1, dp):
        copy = pltpu.make_async_remote_copy(
            src_ref=gain_ref,
            dst_ref=gbuf.at[z],
            send_sem=gsend.at[k],
            recv_sem=grecv.at[k],
            device_id={"dp": lax.rem(z + k, dp)},
            device_id_type=MESH,
        )
        copy.start()
        gcopies.append(copy)

    lax.fori_loop(0, nch + SUM_SKEW * (dp - 1), step, 0)

    for copy in gcopies:
        copy.wait()
    gbuf[pl.ds(z, 1)] = gain_ref[...][None]
    gain_out[...] = jnp.sum(gbuf[...], axis=0)
    squares = jnp.sum(jnp.sum(acc[...], axis=1, keepdims=True), axis=0, keepdims=True)
    sq_out[...] = jnp.broadcast_to(squares, sq_out.shape)

    @pl.when(jnp.logical_and(z > 0, z < dp - 1))
    def _():
        out_ref[...] = jnp.zeros_like(out_ref)

    def drain(c, carry):
        for m in range(MATS):

            @pl.when(hops[m] < dp - 1)
            def _():
                remote(m, c, rbuf, target[m]).wait_send()

        return carry

    lax.fori_loop(0, nch, drain, 0)


def line_sum(dp, grads, gain_grad):
    mats, rows, cols = grads.shape
    ch = chunk_rows(rows, 16)
    nch = rows // ch
    dma = pltpu.SemaphoreType.DMA
    return pl.pallas_call(
        functools.partial(line_sum_kernel, dp, ch),
        out_shape=(
            jax.ShapeDtypeStruct((rows, cols), jnp.float32),
            jax.ShapeDtypeStruct(gain_grad.shape, jnp.float32),
            jax.ShapeDtypeStruct((8, 128), jnp.float32),
        ),
        in_specs=[VMEM, VMEM],
        out_specs=(VMEM, VMEM, VMEM),
        scratch_shapes=[
            pltpu.VMEM((mats, rows, cols), jnp.float32),
            pltpu.VMEM((dp,) + gain_grad.shape, jnp.float32),
            pltpu.VMEM((8, cols), jnp.float32),
            dma((mats, nch)),
            dma((mats, nch)),
            dma((dp,)),
            dma((dp,)),
        ],
        compiler_params=pltpu.CompilerParams(
            collective_id=0, has_side_effects=True, vmem_limit_bytes=40 * 2**20
        ),
    )(grads, gain_grad)


def line_spread_kernel(dp, parts, *refs):
    n = len(parts)
    ins, outs = refs[:n], refs[n : 2 * n]
    send, recv, keep, pair_send, pair_recv = refs[2 * n :]
    z, core = lax.axis_index("dp"), lax.axis_index("tensor")
    barrier = pltpu.get_barrier_semaphore()
    for k in range(1, dp):
        pl.semaphore_signal(
            barrier, inc=1, device_id={"dp": lax.rem(z + k, dp)}, device_id_type=MESH
        )
    pl.semaphore_signal(barrier, inc=1, device_id={"tensor": 1 - core}, device_id_type=MESH)
    pl.semaphore_wait(barrier, dp)
    hops = (z, dp - 1 - z)
    target = (jnp.minimum(z + 1, dp - 1), jnp.maximum(z - 1, 0))
    plan = []
    for a, (rows, ch) in enumerate(parts):
        span = rows // 2 if a == n - 1 else rows
        plan += [(a, r, ch, span) for r in range(0, span, ch)]

    def rows_of(k, owner):
        a, r, ch, span = plan[k]
        if a < n - 1:
            return pl.ds(r, ch)
        return pl.ds(pl.multiple_of(owner * span + r, 8), ch)

    def remote(m, k, first):
        a = plan[k][0]
        rows = rows_of(k, core)
        dst = outs[a].at[m, rows]
        return pltpu.make_async_remote_copy(
            src_ref=ins[a].at[rows] if first else dst,
            dst_ref=dst,
            send_sem=send.at[m, k],
            recv_sem=recv.at[m, k],
            device_id={"dp": target[m]},
            device_id_type=MESH,
        )

    def across(m, k, owner):
        ref = outs[n - 1].at[m, rows_of(k, owner)]
        return pltpu.make_async_remote_copy(
            src_ref=ref,
            dst_ref=ref,
            send_sem=pair_send.at[m, k],
            recv_sem=pair_recv.at[m, k],
            device_id={"tensor": 1 - core},
            device_id_type=MESH,
        )

    split = [k for k in range(len(plan)) if plan[k][0] == n - 1]
    for m in range(MATS):

        @pl.when(hops[m] == 0)
        def _():
            for k in range(len(plan)):
                remote(m, k, True).start()
            for a in range(n):
                pltpu.make_async_copy(ins[a], outs[a].at[m], keep.at[a]).start()

    for i in range(len(plan) + SPREAD_SKEW * (dp - 1)):
        for m in range(MATS):
            for h in range(1, dp):
                k = i - SPREAD_SKEW * h
                if 0 <= k < len(plan):

                    @pl.when(hops[m] == h)
                    def _():
                        remote(m, k, False).wait_recv()
                        if h < dp - 1:
                            remote(m, k, False).start()
                        if k in split:
                            across(m, k, core).start()

    for m in range(MATS):

        @pl.when(hops[m] == 0)
        def _():
            for a in range(n):
                pltpu.make_async_copy(ins[a], outs[a].at[m], keep.at[a]).wait()

        @pl.when(hops[m] > 0)
        def _():
            for k in split:
                across(m, k, core).wait_send()
                across(m, k, 1 - core).wait_recv()

        @pl.when(hops[m] < dp - 1)
        def _():
            for k in range(len(plan)):
                remote(m, k, False).wait_send()


def line_spread(dp, arrays, sizes):
    parts = tuple((a.shape[0], size) for a, size in zip(arrays, sizes))
    nk = sum(a.shape[0] // size for a, size in zip(arrays, sizes))
    dma = pltpu.SemaphoreType.DMA
    return pl.pallas_call(
        functools.partial(line_spread_kernel, dp, parts),
        out_shape=tuple(jax.ShapeDtypeStruct((MATS,) + a.shape, jnp.float32) for a in arrays),
        in_specs=[VMEM] * len(arrays),
        out_specs=tuple(VMEM for _ in arrays),
        scratch_shapes=[dma((MATS, nk))] * 2 + [dma((len(arrays),))] + [dma((MATS, nk))] * 2,
        compiler_params=pltpu.CompilerParams(
            collective_id=1, has_side_effects=True, vmem_limit_bytes=32 * 2**20
        ),
    )(*arrays)


def plane_sum_kernel(
    x_ref, sq_ref, out_ref, sq_out, abuf, hbuf, bbuf, sqbuf, a_sem, b_sem, c_sem, d_sem, s_sem
):
    core, s = lax.axis_index("tensor"), lax.axis_index("shard")
    half = x_ref.shape[0] // 2
    piece = half // 4
    barrier = pltpu.get_barrier_semaphore()
    others = [(lax.rem(core + i, 2), lax.rem(s + k, 4)) for i in range(2) for k in range(4)][1:]
    for c, t in others:
        pl.semaphore_signal(
            barrier, inc=1, device_id={"tensor": c, "shard": t}, device_id_type=MESH
        )
    pl.semaphore_wait(barrier, 7)

    def remote(src, dst, sems, i, device):
        return pltpu.make_async_remote_copy(
            src_ref=src,
            dst_ref=dst,
            send_sem=sems.at[0, i],
            recv_sem=sems.at[1, i],
            device_id=device,
            device_id_type=MESH,
        )

    def rows_at(start):
        return pl.ds(pl.multiple_of(start, 8), piece)

    sibling = {"tensor": 1 - core}
    order = [lax.rem(s + k, 4) for k in (1, 2, 3, 0)]
    pair = []
    for i, t in enumerate(order):
        rows = rows_at(t * piece)
        copy = remote(
            x_ref.at[rows_at((1 - core) * half + t * piece)], abuf.at[rows], a_sem, i, sibling
        )
        copy.start()
        pair.append(copy)
    me = core * 4 + s
    squares = []
    for i, (c, t) in enumerate(others):
        copy = remote(sq_ref, sqbuf.at[me], s_sem, i, {"tensor": c, "shard": t})
        copy.start()
        squares.append(copy)
    spread = []
    for i, t in enumerate(order):
        rows = rows_at(t * piece)
        pair[i].wait_recv()
        hbuf[rows, :] = x_ref[rows_at(core * half + t * piece), :] + abuf[rows, :]
        if i < 3:
            copy = remote(hbuf.at[rows], bbuf.at[i], b_sem, i, {"shard": t})
            copy.start()
            spread.append(copy)
    mine = rows_at(core * half + s * piece)
    for copy in spread:
        copy.wait_recv()
    out_ref[mine, :] = (hbuf[rows_at(s * piece), :] + bbuf[0]) + (bbuf[1] + bbuf[2])
    gather = []
    for i in range(3):
        copy = remote(out_ref.at[mine], out_ref.at[mine], c_sem, i, {"shard": order[i]})
        copy.start()
        gather.append(copy)
    across = [remote(out_ref.at[mine], out_ref.at[mine], d_sem, 3, sibling)]
    across[0].start()
    for i in range(3):
        gather[i].wait_recv()
        rows = rows_at(core * half + lax.rem(s + 3 - i, 4) * piece)
        copy = remote(out_ref.at[rows], out_ref.at[rows], d_sem, i, sibling)
        copy.start()
        across.append(copy)
    for copy in squares:
        copy.wait()
    sqbuf[pl.ds(me, 1)] = sq_ref[...][None]
    sq_out[...] = jnp.sum(sqbuf[...], axis=0)
    for copy in across:
        copy.wait()
    for copy in pair + spread + gather:
        copy.wait_send()


def plane_sum(partial, squares):
    rows, rank = partial.shape
    piece = rows // 8
    dma = pltpu.SemaphoreType.DMA
    return pl.pallas_call(
        plane_sum_kernel,
        out_shape=(
            jax.ShapeDtypeStruct(partial.shape, jnp.float32),
            jax.ShapeDtypeStruct(squares.shape, jnp.float32),
        ),
        in_specs=[VMEM, VMEM],
        out_specs=(VMEM, VMEM),
        scratch_shapes=[
            pltpu.VMEM((rows // 2, rank), jnp.float32),
            pltpu.VMEM((rows // 2, rank), jnp.float32),
            pltpu.VMEM((3, piece, rank), jnp.float32),
            pltpu.VMEM((8,) + squares.shape, jnp.float32),
            dma((2, 4)),
            dma((2, 3)),
            dma((2, 3)),
            dma((2, 4)),
            dma((2, 7)),
        ],
        compiler_params=pltpu.CompilerParams(collective_id=2, has_side_effects=True),
    )(partial, squares)


def gather_kernel(ch, rate, delta_ref, w_ref, out_ref, rbuf, own_sem, fwd_sem, recv_sem):
    s = lax.axis_index("shard")
    y, x = s // 2, lax.rem(s, 2)
    source = (y * 2 + (1 - x), (1 - y) * 2 + x, (1 - y) * 2 + (1 - x))
    barrier = pltpu.get_barrier_semaphore()
    for r in range(2):
        pl.semaphore_signal(barrier, inc=1, device_id={"shard": source[r]}, device_id_type=MESH)
    pl.semaphore_wait(barrier, 2)
    mats, rows, cols = delta_ref.shape
    per = rows // ch
    nch = mats * per

    def place(ref, j):
        return ref.at[j // per, pl.ds(pl.multiple_of(lax.rem(j, per) * ch, 8), ch)]

    def own(r, j):
        return pltpu.make_async_remote_copy(
            src_ref=place(delta_ref, j),
            dst_ref=place(rbuf.at[r], j),
            send_sem=own_sem.at[r, j],
            recv_sem=recv_sem.at[r, j],
            device_id={"shard": source[r]},
            device_id_type=MESH,
        )

    def forward(r, j):
        return pltpu.make_async_remote_copy(
            src_ref=place(rbuf.at[1 - r], j),
            dst_ref=place(rbuf.at[2], j),
            send_sem=fwd_sem.at[j],
            recv_sem=recv_sem.at[2, j],
            device_id={"shard": source[r]},
            device_id_type=MESH,
        )

    def start(j, carry):
        for r in range(2):
            own(r, j).start()
        return carry

    lax.fori_loop(0, nch, start, 0)

    def write(j, src, chunk):
        m = j // per
        at = pl.ds(pl.multiple_of(lax.rem(j, per) * ch, 8), ch)
        for t in range(4):

            @pl.when(src == t)
            def _():
                lanes = slice(t * cols, (t + 1) * cols)
                out_ref[m, at, lanes] = w_ref[m, at, lanes] - rate * chunk[...]

    def near(j, carry):
        for r in range(2):
            own(r, j).wait_recv()
        for r in range(2):

            @pl.when(lax.rem(j, 2) == r)
            def _():
                forward(r, j).start()

        write(j, s, place(delta_ref, j))
        for r in range(2):
            write(j, source[r], place(rbuf.at[r], j))
        return carry

    lax.fori_loop(0, nch, near, 0)

    def far(j, carry):
        forward(0, j).wait()
        write(j, source[2], place(rbuf.at[2], j))
        for r in range(2):
            own(r, j).wait_send()
        return carry

    lax.fori_loop(0, nch, far, 0)


def gather_update(delta, weights, rate):
    mats, rows, cols = delta.shape
    ch = chunk_rows(rows, 32)
    nch = mats * (rows // ch)
    dma = pltpu.SemaphoreType.DMA
    return pl.pallas_call(
        functools.partial(gather_kernel, ch, rate),
        out_shape=jax.ShapeDtypeStruct(weights.shape, jnp.float32),
        in_specs=[VMEM, VMEM],
        out_specs=VMEM,
        scratch_shapes=[
            pltpu.VMEM((3, mats, rows, cols), jnp.float32),
            dma((2, nch)),
            dma((nch,)),
            dma((3, nch)),
        ],
        compiler_params=pltpu.CompilerParams(
            collective_id=3, has_side_effects=True, vmem_limit_bytes=40 * 2**20
        ),
    )(delta, weights)


def per_device(
    dp,
    weights,
    grads,
    bases,
    first_moment,
    second_moment,
    gain,
    gain_grad,
    gain_first,
    gain_second,
):
    z = lax.axis_index("dp")
    shards = lax.axis_size("shard")
    ff = first_moment.shape[2] * lax.axis_size("tensor") * shards
    mine, gain_total, squares = line_sum(dp, jnp.swapaxes(grads[0], 1, 2), gain_grad)
    gain_total = gain_total[0]
    basis = lax.dynamic_index_in_dim(bases, jnp.where(z * 2 >= dp, 1, 0), 0, keepdims=False)
    rows, rank = basis.shape
    carried = dot(mine, basis, ((1,), (0,)))
    partial = dot(mine, carried, ((0,), (0,)))
    direct = shards == 4 and lax.axis_size("tensor") == 2 and rows % 64 == 0
    if direct:
        sketch, squares = plane_sum(partial, squares)
    else:
        sketch, squares = lax.psum((partial, squares), ("tensor", "shard"))
    iterate = sketch / (jnp.sqrt(jnp.sum(sketch * sketch)) + norm_eps)
    gram = dot(iterate, iterate, ((0,), (0,)))
    eye = jnp.eye(rank, dtype=jnp.float32)
    product = None
    for turn in range(NS_STEPS):
        factor = 1.5 * eye - 0.5 * gram
        product = factor if product is None else dot(product, factor, ((1,), (0,)))
        if turn < NS_STEPS - 1:
            gram = dot(dot(factor, gram, ((1,), (0,))), factor, ((1,), (0,)))
    new_basis = dot(iterate, product, ((1,), (0,)))
    projected = dot(mine, new_basis, ((1,), (0,)))
    projected, squares, new_bases = line_spread(
        dp,
        (projected, squares, new_basis),
        (chunk_rows(projected.shape[0], 32), 8, chunk_rows(rows // 2, 64)),
    )

    total_squares = squares[0, 0, 0] + squares[1, 0, 0] + jnp.sum(gain_total * gain_total)
    clip_factor = jnp.minimum(1.0, math.sqrt(MATS * ff) / (jnp.sqrt(total_squares) + norm_eps))
    bias_one = 1.0 - beta_one**adam_step
    bias_two = 1.0 - beta_two**adam_step
    projected_gradient = clip_factor * projected
    new_first = beta_one * jnp.swapaxes(first_moment, 1, 2) + (1.0 - beta_one) * projected_gradient
    new_second = (
        beta_two * jnp.swapaxes(second_moment, 1, 2)
        + (1.0 - beta_two) * projected_gradient * projected_gradient
    )
    direction = new_first / bias_one / (jnp.sqrt(new_second / bias_two) + adam_eps)
    new_first, new_second = jnp.swapaxes(new_first, 1, 2), jnp.swapaxes(new_second, 1, 2)
    row_count = weights.shape[1]
    slab = lax.dynamic_slice_in_dim(new_bases, z * row_count, row_count, 1)
    delta = lax.dot_general(
        slab,
        direction,
        (((2,), (2,)), ((0,), (0,))),
        precision=lax.Precision.HIGH,
        preferred_element_type=jnp.float32,
    )
    if direct:
        new_weights = gather_update(delta, weights, learn_rate * galore_scale)
    else:
        delta = lax.all_gather(delta, "shard", axis=2, tiled=True)
        new_weights = weights - learn_rate * galore_scale * delta
    clipped_gain = clip_factor * gain_total
    gain_first_new = beta_one * gain_first + (1.0 - beta_one) * clipped_gain
    gain_second_new = beta_two * gain_second + (1.0 - beta_two) * clipped_gain * clipped_gain
    gain_new = gain - learn_rate * (gain_first_new / bias_one) / (
        jnp.sqrt(gain_second_new / bias_two) + adam_eps
    )
    return (
        new_weights,
        new_bases,
        new_first,
        new_second,
        gain_new,
        gain_first_new,
        gain_second_new,
    )


def solution(mesh):
    placed = (
        P(None, "dp", "tensor"),
        P("dp", None, None, ("tensor", "shard")),
        P(),
        P(None, None, ("tensor", "shard")),
        P(None, None, ("tensor", "shard")),
        P(),
        P("dp", None),
        P(),
        P(),
    )
    return jax.shard_map(
        functools.partial(per_device, mesh.shape["dp"]),
        mesh=mesh,
        in_specs=placed,
        out_specs=(
            P(None, "dp", "tensor"),
            P(),
            P(None, None, ("tensor", "shard")),
            P(None, None, ("tensor", "shard")),
            P(),
            P(),
            P(),
        ),
        check_vma=False,
    )
```

```python
import functools
import math

import jax
import jax.numpy as jnp
from jax import lax
from jax.experimental import pallas as pl
from jax.experimental.pallas import tpu as pltpu
from jax.sharding import PartitionSpec as P

NS_STEPS = 5
MATS = 2

beta_one = 0.9
beta_two = 0.999
adam_eps = 1e-08
adam_step = 100
learn_rate = 0.02
galore_scale = 0.25
norm_eps = 1e-06

MESH = pl.DeviceIdType.MESH
VMEM = pl.BlockSpec(memory_space=pltpu.VMEM)
SUM_SKEW = 4
SPREAD_SKEW = 2


def dot(left, right, dims, precision=lax.Precision.HIGH):
    return lax.dot_general(
        left, right, (dims, ((), ())), precision=precision, preferred_element_type=jnp.float32
    )


def greet_line(dp, z):
    barrier = pltpu.get_barrier_semaphore()
    for k in range(1, dp):
        pl.semaphore_signal(
            barrier, inc=1, device_id={"dp": lax.rem(z + k, dp)}, device_id_type=MESH
        )
    pl.semaphore_wait(barrier, dp - 1)


def chunk_rows(rows, want):
    best = 8
    for size in range(8, want + 1, 8):
        if rows % size == 0:
            best = size
    return best


def line_sum_kernel(
    dp, ch, g_ref, gain_ref, out_ref, gain_out, sq_out, rbuf, gbuf, acc, send, recv, gsend, grecv
):
    z = lax.axis_index("dp")
    nch = g_ref.shape[1] // ch
    greet_line(dp, z)

    def remote(m, c, src, target):
        rows = pl.ds(c * ch, ch)
        return pltpu.make_async_remote_copy(
            src_ref=src.at[m, rows],
            dst_ref=rbuf.at[m, rows],
            send_sem=send.at[m, c],
            recv_sem=recv.at[m, c],
            device_id={"dp": target},
            device_id_type=MESH,
        )

    hops = (dp - 1 - z, z)
    target = (jnp.maximum(z - 1, 0), jnp.minimum(z + 1, dp - 1))

    def step(i, carry):
        for m in range(MATS):
            c = i - SUM_SKEW * hops[m]
            live = jnp.logical_and(c >= 0, c < nch)
            rows = pl.ds(pl.multiple_of(c * ch, 8), ch)

            @pl.when(jnp.logical_and(live, hops[m] == 0))
            def _():
                remote(m, c, g_ref, target[m]).start()

            @pl.when(jnp.logical_and(live, hops[m] > 0))
            def _():
                remote(m, c, rbuf, target[m]).wait_recv()

            @pl.when(jnp.logical_and(live, jnp.logical_and(hops[m] > 0, hops[m] < dp - 1)))
            def _():
                rbuf[m, rows, :] = rbuf[m, rows, :] + g_ref[m, rows, :]
                remote(m, c, rbuf, target[m]).start()

            @pl.when(jnp.logical_and(live, hops[m] == dp - 1))
            def _():
                total = rbuf[m, rows, :] + g_ref[m, rows, :]
                out_ref[rows, :] = total
                for r in range(0, ch, 8):
                    acc[...] += total[r : r + 8] * total[r : r + 8]

        return carry

    acc[...] = jnp.zeros_like(acc)
    gcopies = []
    for k in range(1, dp):
        copy = pltpu.make_async_remote_copy(
            src_ref=gain_ref,
            dst_ref=gbuf.at[z],
            send_sem=gsend.at[k],
            recv_sem=grecv.at[k],
            device_id={"dp": lax.rem(z + k, dp)},
            device_id_type=MESH,
        )
        copy.start()
        gcopies.append(copy)

    lax.fori_loop(0, nch + SUM_SKEW * (dp - 1), step, 0)

    for copy in gcopies:
        copy.wait()
    gbuf[pl.ds(z, 1)] = gain_ref[...][None]
    gain_out[...] = jnp.sum(gbuf[...], axis=0)
    squares = jnp.sum(jnp.sum(acc[...], axis=1, keepdims=True), axis=0, keepdims=True)
    sq_out[...] = jnp.broadcast_to(squares, sq_out.shape)

    @pl.when(jnp.logical_and(z > 0, z < dp - 1))
    def _():
        out_ref[...] = jnp.zeros_like(out_ref)

    def drain(c, carry):
        for m in range(MATS):

            @pl.when(hops[m] < dp - 1)
            def _():
                remote(m, c, rbuf, target[m]).wait_send()

        return carry

    lax.fori_loop(0, nch, drain, 0)


def line_sum(dp, grads, gain_grad):
    mats, rows, cols = grads.shape
    ch = chunk_rows(rows, 16)
    nch = rows // ch
    dma = pltpu.SemaphoreType.DMA
    return pl.pallas_call(
        functools.partial(line_sum_kernel, dp, ch),
        out_shape=(
            jax.ShapeDtypeStruct((rows, cols), jnp.float32),
            jax.ShapeDtypeStruct(gain_grad.shape, jnp.float32),
            jax.ShapeDtypeStruct((8, 128), jnp.float32),
        ),
        in_specs=[VMEM, VMEM],
        out_specs=(VMEM, VMEM, VMEM),
        scratch_shapes=[
            pltpu.VMEM((mats, rows, cols), jnp.float32),
            pltpu.VMEM((dp,) + gain_grad.shape, jnp.float32),
            pltpu.VMEM((8, cols), jnp.float32),
            dma((mats, nch)),
            dma((mats, nch)),
            dma((dp,)),
            dma((dp,)),
        ],
        compiler_params=pltpu.CompilerParams(
            collective_id=0, has_side_effects=True, vmem_limit_bytes=40 * 2**20
        ),
    )(grads, gain_grad)


def line_spread_kernel(dp, parts, *refs):
    n = len(parts)
    ins, outs = refs[:n], refs[n : 2 * n]
    send, recv, keep, pair_send, pair_recv = refs[2 * n :]
    z, core = lax.axis_index("dp"), lax.axis_index("tensor")
    barrier = pltpu.get_barrier_semaphore()
    for k in range(1, dp):
        pl.semaphore_signal(
            barrier, inc=1, device_id={"dp": lax.rem(z + k, dp)}, device_id_type=MESH
        )
    pl.semaphore_signal(barrier, inc=1, device_id={"tensor": 1 - core}, device_id_type=MESH)
    pl.semaphore_wait(barrier, dp)
    hops = (z, dp - 1 - z)
    target = (jnp.minimum(z + 1, dp - 1), jnp.maximum(z - 1, 0))
    plan = []
    for a, (rows, ch) in enumerate(parts):
        span = rows // 2 if a == n - 1 else rows
        plan += [(a, r, ch, span) for r in range(0, span, ch)]

    def rows_of(k, owner):
        a, r, ch, span = plan[k]
        if a < n - 1:
            return pl.ds(r, ch)
        return pl.ds(pl.multiple_of(owner * span + r, 8), ch)

    def remote(m, k, first):
        a = plan[k][0]
        rows = rows_of(k, core)
        dst = outs[a].at[m, rows]
        return pltpu.make_async_remote_copy(
            src_ref=ins[a].at[rows] if first else dst,
            dst_ref=dst,
            send_sem=send.at[m, k],
            recv_sem=recv.at[m, k],
            device_id={"dp": target[m]},
            device_id_type=MESH,
        )

    def across(m, k, owner):
        ref = outs[n - 1].at[m, rows_of(k, owner)]
        return pltpu.make_async_remote_copy(
            src_ref=ref,
            dst_ref=ref,
            send_sem=pair_send.at[m, k],
            recv_sem=pair_recv.at[m, k],
            device_id={"tensor": 1 - core},
            device_id_type=MESH,
        )

    split = [k for k in range(len(plan)) if plan[k][0] == n - 1]
    for m in range(MATS):

        @pl.when(hops[m] == 0)
        def _():
            for k in range(len(plan)):
                remote(m, k, True).start()
            for a in range(n):
                pltpu.make_async_copy(ins[a], outs[a].at[m], keep.at[a]).start()

    for i in range(len(plan) + SPREAD_SKEW * (dp - 1)):
        for m in range(MATS):
            for h in range(1, dp):
                k = i - SPREAD_SKEW * h
                if 0 <= k < len(plan):

                    @pl.when(hops[m] == h)
                    def _():
                        remote(m, k, False).wait_recv()
                        if h < dp - 1:
                            remote(m, k, False).start()
                        if k in split:
                            across(m, k, core).start()

    for m in range(MATS):

        @pl.when(hops[m] == 0)
        def _():
            for a in range(n):
                pltpu.make_async_copy(ins[a], outs[a].at[m], keep.at[a]).wait()

        @pl.when(hops[m] > 0)
        def _():
            for k in split:
                across(m, k, core).wait_send()
                across(m, k, 1 - core).wait_recv()

        @pl.when(hops[m] < dp - 1)
        def _():
            for k in range(len(plan)):
                remote(m, k, False).wait_send()


def line_spread(dp, arrays, sizes):
    parts = tuple((a.shape[0], size) for a, size in zip(arrays, sizes))
    nk = sum(a.shape[0] // size for a, size in zip(arrays, sizes))
    dma = pltpu.SemaphoreType.DMA
    return pl.pallas_call(
        functools.partial(line_spread_kernel, dp, parts),
        out_shape=tuple(jax.ShapeDtypeStruct((MATS,) + a.shape, jnp.float32) for a in arrays),
        in_specs=[VMEM] * len(arrays),
        out_specs=tuple(VMEM for _ in arrays),
        scratch_shapes=[dma((MATS, nk))] * 2 + [dma((len(arrays),))] + [dma((MATS, nk))] * 2,
        compiler_params=pltpu.CompilerParams(
            collective_id=1, has_side_effects=True, vmem_limit_bytes=32 * 2**20
        ),
    )(*arrays)


def plane_sum_kernel(
    x_ref, sq_ref, out_ref, sq_out, abuf, hbuf, bbuf, sqbuf, a_sem, b_sem, c_sem, d_sem, s_sem
):
    core, s = lax.axis_index("tensor"), lax.axis_index("shard")
    half = x_ref.shape[0] // 2
    piece = half // 4
    barrier = pltpu.get_barrier_semaphore()
    others = [(lax.rem(core + i, 2), lax.rem(s + k, 4)) for i in range(2) for k in range(4)][1:]
    for c, t in others:
        pl.semaphore_signal(
            barrier, inc=1, device_id={"tensor": c, "shard": t}, device_id_type=MESH
        )
    pl.semaphore_wait(barrier, 7)

    def remote(src, dst, sems, i, device):
        return pltpu.make_async_remote_copy(
            src_ref=src,
            dst_ref=dst,
            send_sem=sems.at[0, i],
            recv_sem=sems.at[1, i],
            device_id=device,
            device_id_type=MESH,
        )

    def rows_at(start):
        return pl.ds(pl.multiple_of(start, 8), piece)

    sibling = {"tensor": 1 - core}
    order = [lax.rem(s + k, 4) for k in (1, 2, 3, 0)]
    pair = []
    for i, t in enumerate(order):
        rows = rows_at(t * piece)
        copy = remote(
            x_ref.at[rows_at((1 - core) * half + t * piece)], abuf.at[rows], a_sem, i, sibling
        )
        copy.start()
        pair.append(copy)
    me = core * 4 + s
    squares = []
    for i, (c, t) in enumerate(others):
        copy = remote(sq_ref, sqbuf.at[me], s_sem, i, {"tensor": c, "shard": t})
        copy.start()
        squares.append(copy)
    spread = []
    for i, t in enumerate(order):
        rows = rows_at(t * piece)
        pair[i].wait_recv()
        hbuf[rows, :] = x_ref[rows_at(core * half + t * piece), :] + abuf[rows, :]
        if i < 3:
            copy = remote(hbuf.at[rows], bbuf.at[i], b_sem, i, {"shard": t})
            copy.start()
            spread.append(copy)
    mine = rows_at(core * half + s * piece)
    for copy in spread:
        copy.wait_recv()
    out_ref[mine, :] = (hbuf[rows_at(s * piece), :] + bbuf[0]) + (bbuf[1] + bbuf[2])
    gather = []
    for i in range(3):
        copy = remote(out_ref.at[mine], out_ref.at[mine], c_sem, i, {"shard": order[i]})
        copy.start()
        gather.append(copy)
    across = [remote(out_ref.at[mine], out_ref.at[mine], d_sem, 3, sibling)]
    across[0].start()
    for i in range(3):
        gather[i].wait_recv()
        rows = rows_at(core * half + lax.rem(s + 3 - i, 4) * piece)
        copy = remote(out_ref.at[rows], out_ref.at[rows], d_sem, i, sibling)
        copy.start()
        across.append(copy)
    for copy in squares:
        copy.wait()
    sqbuf[pl.ds(me, 1)] = sq_ref[...][None]
    sq_out[...] = jnp.sum(sqbuf[...], axis=0)
    for copy in across:
        copy.wait()
    for copy in pair + spread + gather:
        copy.wait_send()


def plane_sum(partial, squares):
    rows, rank = partial.shape
    piece = rows // 8
    dma = pltpu.SemaphoreType.DMA
    return pl.pallas_call(
        plane_sum_kernel,
        out_shape=(
            jax.ShapeDtypeStruct(partial.shape, jnp.float32),
            jax.ShapeDtypeStruct(squares.shape, jnp.float32),
        ),
        in_specs=[VMEM, VMEM],
        out_specs=(VMEM, VMEM),
        scratch_shapes=[
            pltpu.VMEM((rows // 2, rank), jnp.float32),
            pltpu.VMEM((rows // 2, rank), jnp.float32),
            pltpu.VMEM((3, piece, rank), jnp.float32),
            pltpu.VMEM((8,) + squares.shape, jnp.float32),
            dma((2, 4)),
            dma((2, 3)),
            dma((2, 3)),
            dma((2, 4)),
            dma((2, 7)),
        ],
        compiler_params=pltpu.CompilerParams(collective_id=2, has_side_effects=True),
    )(partial, squares)


def gather_kernel(ch, rate, delta_ref, w_ref, out_ref, rbuf, own_sem, fwd_sem, recv_sem):
    s = lax.axis_index("shard")
    y, x = s // 2, lax.rem(s, 2)
    source = (y * 2 + (1 - x), (1 - y) * 2 + x, (1 - y) * 2 + (1 - x))
    barrier = pltpu.get_barrier_semaphore()
    for r in range(2):
        pl.semaphore_signal(barrier, inc=1, device_id={"shard": source[r]}, device_id_type=MESH)
    pl.semaphore_wait(barrier, 2)
    mats, rows, cols = delta_ref.shape
    per = rows // ch
    nch = mats * per

    def place(ref, j):
        return ref.at[j // per, pl.ds(pl.multiple_of(lax.rem(j, per) * ch, 8), ch)]

    def own(r, j):
        return pltpu.make_async_remote_copy(
            src_ref=place(delta_ref, j),
            dst_ref=place(rbuf.at[r], j),
            send_sem=own_sem.at[r, j],
            recv_sem=recv_sem.at[r, j],
            device_id={"shard": source[r]},
            device_id_type=MESH,
        )

    def forward(r, j):
        return pltpu.make_async_remote_copy(
            src_ref=place(rbuf.at[1 - r], j),
            dst_ref=place(rbuf.at[2], j),
            send_sem=fwd_sem.at[j],
            recv_sem=recv_sem.at[2, j],
            device_id={"shard": source[r]},
            device_id_type=MESH,
        )

    def start(j, carry):
        for r in range(2):
            own(r, j).start()
        return carry

    lax.fori_loop(0, nch, start, 0)

    def write(j, src, chunk):
        m = j // per
        at = pl.ds(pl.multiple_of(lax.rem(j, per) * ch, 8), ch)
        for t in range(4):

            @pl.when(src == t)
            def _():
                lanes = slice(t * cols, (t + 1) * cols)
                out_ref[m, at, lanes] = w_ref[m, at, lanes] - rate * chunk[...]

    def near(j, carry):
        for r in range(2):
            own(r, j).wait_recv()
        for r in range(2):

            @pl.when(lax.rem(j, 2) == r)
            def _():
                forward(r, j).start()

        write(j, s, place(delta_ref, j))
        for r in range(2):
            write(j, source[r], place(rbuf.at[r], j))
        return carry

    lax.fori_loop(0, nch, near, 0)

    def far(j, carry):
        forward(0, j).wait()
        write(j, source[2], place(rbuf.at[2], j))
        for r in range(2):
            own(r, j).wait_send()
        return carry

    lax.fori_loop(0, nch, far, 0)


def gather_update(delta, weights, rate):
    mats, rows, cols = delta.shape
    ch = chunk_rows(rows, 32)
    nch = mats * (rows // ch)
    dma = pltpu.SemaphoreType.DMA
    return pl.pallas_call(
        functools.partial(gather_kernel, ch, rate),
        out_shape=jax.ShapeDtypeStruct(weights.shape, jnp.float32),
        in_specs=[VMEM, VMEM],
        out_specs=VMEM,
        scratch_shapes=[
            pltpu.VMEM((3, mats, rows, cols), jnp.float32),
            dma((2, nch)),
            dma((nch,)),
            dma((3, nch)),
        ],
        compiler_params=pltpu.CompilerParams(
            collective_id=3, has_side_effects=True, vmem_limit_bytes=40 * 2**20
        ),
    )(delta, weights)


def per_device(
    dp,
    weights,
    grads,
    bases,
    first_moment,
    second_moment,
    gain,
    gain_grad,
    gain_first,
    gain_second,
):
    z = lax.axis_index("dp")
    shards = lax.axis_size("shard")
    ff = first_moment.shape[2] * lax.axis_size("tensor") * shards
    mine, gain_total, squares = line_sum(dp, jnp.swapaxes(grads[0], 1, 2), gain_grad)
    gain_total = gain_total[0]
    basis = lax.dynamic_index_in_dim(bases, jnp.where(z * 2 >= dp, 1, 0), 0, keepdims=False)
    rows, rank = basis.shape
    carried = dot(mine, basis, ((1,), (0,)))
    partial = dot(mine, carried, ((0,), (0,)))
    direct = shards == 4 and lax.axis_size("tensor") == 2 and rows % 64 == 0
    if direct:
        sketch, squares = plane_sum(partial, squares)
    else:
        sketch, squares = lax.psum((partial, squares), ("tensor", "shard"))
    iterate = sketch / (jnp.sqrt(jnp.sum(sketch * sketch)) + norm_eps)
    gram = dot(iterate, iterate, ((0,), (0,)))
    eye = jnp.eye(rank, dtype=jnp.float32)
    product = None
    for turn in range(NS_STEPS):
        factor = 1.5 * eye - 0.5 * gram
        product = factor if product is None else dot(product, factor, ((1,), (0,)))
        if turn < NS_STEPS - 1:
            gram = dot(dot(factor, gram, ((1,), (0,))), factor, ((1,), (0,)))
    new_basis = dot(iterate, product, ((1,), (0,)))
    projected = dot(mine, new_basis, ((1,), (0,)))
    projected, squares, new_bases = line_spread(
        dp,
        (projected, squares, new_basis),
        (chunk_rows(projected.shape[0], 152), 8, chunk_rows(rows // 2, 112)),
    )

    total_squares = squares[0, 0, 0] + squares[1, 0, 0] + jnp.sum(gain_total * gain_total)
    clip_factor = jnp.minimum(1.0, math.sqrt(MATS * ff) / (jnp.sqrt(total_squares) + norm_eps))
    bias_one = 1.0 - beta_one**adam_step
    bias_two = 1.0 - beta_two**adam_step
    projected_gradient = clip_factor * projected
    new_first = beta_one * jnp.swapaxes(first_moment, 1, 2) + (1.0 - beta_one) * projected_gradient
    new_second = (
        beta_two * jnp.swapaxes(second_moment, 1, 2)
        + (1.0 - beta_two) * projected_gradient * projected_gradient
    )
    direction = new_first / bias_one / (jnp.sqrt(new_second / bias_two) + adam_eps)
    new_first, new_second = jnp.swapaxes(new_first, 1, 2), jnp.swapaxes(new_second, 1, 2)
    row_count = weights.shape[1]
    slab = lax.dynamic_slice_in_dim(new_bases, z * row_count, row_count, 1)
    delta = lax.dot_general(
        slab,
        direction,
        (((2,), (2,)), ((0,), (0,))),
        precision=lax.Precision.HIGH,
        preferred_element_type=jnp.float32,
    )
    if direct:
        new_weights = gather_update(delta, weights, learn_rate * galore_scale)
    else:
        delta = lax.all_gather(delta, "shard", axis=2, tiled=True)
        new_weights = weights - learn_rate * galore_scale * delta
    clipped_gain = clip_factor * gain_total
    gain_first_new = beta_one * gain_first + (1.0 - beta_one) * clipped_gain
    gain_second_new = beta_two * gain_second + (1.0 - beta_two) * clipped_gain * clipped_gain
    gain_new = gain - learn_rate * (gain_first_new / bias_one) / (
        jnp.sqrt(gain_second_new / bias_two) + adam_eps
    )
    return (
        new_weights,
        new_bases,
        new_first,
        new_second,
        gain_new,
        gain_first_new,
        gain_second_new,
    )


def solution(mesh):
    placed = (
        P(None, "dp", "tensor"),
        P("dp", None, None, ("tensor", "shard")),
        P(),
        P(None, None, ("tensor", "shard")),
        P(None, None, ("tensor", "shard")),
        P(),
        P("dp", None),
        P(),
        P(),
    )
    return jax.shard_map(
        functools.partial(per_device, mesh.shape["dp"]),
        mesh=mesh,
        in_specs=placed,
        out_specs=(
            P(None, "dp", "tensor"),
            P(),
            P(None, None, ("tensor", "shard")),
            P(None, None, ("tensor", "shard")),
            P(),
            P(),
            P(),
        ),
        check_vma=False,
    )
```
